1024 devices in a mesh: enc: 32 (over z), llm: 4 (over x), tp: 8 (over y, core).
Axes of the slice: x: 4, y: 4, z: 32, core: 2. Of those that a mesh axis runs over, the one named last changes fastest.
Arguments:
- visual: bfloat16 [32, 4, 32, 4, 8192], P('enc', 'llm'), may hold values from -6 to 6
- counts: int32 [32, 4, 32], P('enc', 'llm'), may hold values from 0 to 4, as said below
- merger_bias: float32 [8192], replicated, may hold values from -3 to 3
- norm_gain: float32 [8192], replicated, may hold values from 0.1 to 1.9
- kv_weight: bfloat16 [8192, 2048], P(None, 'tp'), may hold values from -0.0625 to 0.0625
- kv_cotangent: bfloat16 [32, 4, 32, 4, 2048], P('enc', 'llm', None, None, 'tp'), may hold values from -6 to 6
Outputs:
- key_values: bfloat16 [32, 4, 32, 4, 2048], P('enc', 'llm', None, None, 'tp')
- visual_grad: bfloat16 [32, 4, 32, 4, 8192], P('enc', 'llm', None, None, 'tp')
- bias_grad: float32 [8192], P('tp')
The draws below stay inside these ranges and needn't reach their ends.
Inputs may be any that keep to these rules, and one draw needn't show every extreme that they name: Slots c < counts[s, g, b] of block (s, g, b) hold live merged patch blocks, the others hold unused data. For every group g some bucket b receives 4 live slots from every source s.
All inputs are finite; a program needn't handle non-finite values.
Results may differ from the reference program's by a relative error of at most 0.0049.
Values may be sent and summed in bfloat16 or wider, within the bound.
A program may use at most 64 MiB of HBM per device.

```python
import jax
import jax.numpy as jnp
from jax import lax

D = 8192
CAP = 4
KVD = 2048
N_ENC = 32
N_LLM = 4


def draw_counts(key, part):
    first_key, second_key = jax.random.split(jax.random.fold_in(key, 7))
    base = jax.random.randint(first_key, (N_ENC, N_LLM, N_ENC), 0, CAP + 1)
    full_bucket = jax.random.randint(second_key, (N_LLM,), 0, N_ENC)
    chosen = jnp.arange(N_ENC)[None, :] == full_bucket[:, None]
    return jnp.where(chosen[None, :, :], CAP, base).astype(jnp.int32)


def levels(stream_key, shape, cuts, least, top_value):
    gain, own = 1.0, jax.random.fold_in(stream_key, 6)
    for dim, blocks in cuts:
        steps = jnp.exp(jax.random.uniform(jax.random.fold_in(own, dim), (blocks,), jnp.float32, least / len(cuts), top_value / len(cuts)))
        gain = gain * jnp.repeat(steps, shape[dim] // blocks).reshape([-1 if axis == dim else 1 for axis in range(len(shape))])
    return gain


def scatter_about(rng, dims, scale, reach, cuts=(), kind=jnp.bfloat16):
    entries = jax.random.normal(rng, dims, jnp.float32) * scale
    if len(cuts) > 0:
        entries = levels(rng, dims, cuts, -0.22, 0.18) * entries
    return jnp.clip(entries, min=-reach, max=reach).astype(kind)


def setup_inputs(seed: int = 0) -> dict:
    key_of = jax.random.split(jax.random.key(seed), 7)
    visual = scatter_about(key_of[0], (N_ENC, N_LLM, N_ENC, CAP, D), 1.0, 6.0, ((0, 32), (1, 4)))
    counts = draw_counts(jax.random.fold_in(key_of[6], 71), 0)
    merger_bias = scatter_about(key_of[2], (D,), 0.5, 3.0, (), jnp.float32)
    norm_gain = jnp.clip(1.0 + 0.18 * jax.random.normal(key_of[3], (D,), jnp.float32), 0.1, 1.9)
    kv_weight = scatter_about(key_of[4], (D, KVD), D ** -0.5, 0.0625, ((1, 8),))
    kv_cotangent = scatter_about(key_of[5], (N_ENC, N_LLM, N_ENC, CAP, KVD), 1.0, 6.0, ((0, 32), (1, 4), (4, 8)))
    return dict(visual=visual, counts=counts, merger_bias=merger_bias, norm_gain=norm_gain, kv_weight=kv_weight, kv_cotangent=kv_cotangent)


def reference(visual, counts, merger_bias, norm_gain, kv_weight, kv_cotangent):
    features = visual.shape[4]
    columns = kv_weight.shape[1]
    bucketed = jnp.transpose(visual, (2, 1, 0, 3, 4))
    bucket_counts = jnp.transpose(counts, (2, 1, 0))

    def per_bucket(pieces):
        slot_rows, slot_counts, cot_rows = pieces
        live = lax.broadcasted_iota(jnp.int32, cot_rows.shape[:3], 2) < slot_counts[:, :, None]
        inputs = slot_rows.astype(jnp.float32) + merger_bias
        inv_rms = lax.rsqrt(lax.optimization_barrier(jnp.mean(inputs * inputs, axis=-1, keepdims=True)) + 1e-06)
        normed = (inputs * inv_rms * norm_gain).astype(jnp.bfloat16)
        projected = jnp.dot(normed.reshape(-1, features), kv_weight, preferred_element_type=jnp.float32).reshape(cot_rows.shape)
        live_cols = live[..., None]
        key_out = jnp.where(live_cols, projected, jnp.zeros_like(projected)).astype(jnp.bfloat16)
        masked = jnp.where(live_cols, cot_rows, jnp.zeros_like(cot_rows))
        row_dot = lax.optimization_barrier(jnp.sum(masked.astype(jnp.float32) * projected, axis=-1, keepdims=True))
        grad_normed = lax.dot_general(masked.reshape(-1, columns), kv_weight, (((1,), (1,)), ((), ())), preferred_element_type=jnp.float32).reshape(inputs.shape)
        grad_rows = inv_rms * norm_gain * grad_normed - inputs * (inv_rms * inv_rms) * row_dot / features
        return (key_out, grad_rows.astype(jnp.bfloat16), lax.optimization_barrier(jnp.sum(grad_rows, axis=(0, 1, 2))))
    key_values, grad_bucketed, bias_parts = lax.map(per_bucket, (bucketed, bucket_counts, kv_cotangent))
    visual_grad = jnp.transpose(grad_bucketed, (2, 1, 0, 3, 4))
    return (key_values, visual_grad, lax.optimization_barrier(jnp.sum(bias_parts, axis=0)))
```

```python
import jax
import jax.numpy as jnp
from jax import lax
from jax.sharding import PartitionSpec as P


def per_device(visual, counts, merger_bias, norm_gain, kv_weight, kv_cotangent):
    buckets, capacity, features = visual.shape[2:]
    tp_count = lax.axis_size("tp")
    own_width = features // tp_count
    own_start = lax.axis_index("tp") * own_width
    columns = kv_weight.shape[1]
    rows = buckets * capacity
    cot_rows = lax.all_to_all(
        kv_cotangent[0, 0], "enc", split_axis=0, concat_axis=0, tiled=True
    ).reshape(rows, columns)
    live = (
        lax.broadcasted_iota(jnp.int32, (buckets, capacity), 1) < counts[0, 0][:, None]
    ).reshape(rows, 1)
    inputs = visual[0, 0].reshape(rows, features).astype(jnp.float32) + merger_bias
    inv_rms = lax.rsqrt(jnp.mean(inputs * inputs, axis=1, keepdims=True) + 1e-06)
    normed = (inputs * inv_rms * norm_gain).astype(jnp.bfloat16)
    projected = jnp.dot(normed, kv_weight, preferred_element_type=jnp.float32)
    key_out = jnp.where(live, projected, jnp.zeros_like(projected)).astype(jnp.bfloat16)
    key_values = lax.all_to_all(
        key_out.reshape(buckets, capacity, columns), "enc", split_axis=0, concat_axis=0, tiled=True
    )
    masked = jnp.where(live, cot_rows, jnp.zeros_like(cot_rows))
    part_dots = jnp.sum(masked.astype(jnp.float32) * projected, axis=1, keepdims=True)
    grad_part = lax.dot_general(
        masked, kv_weight, (((1,), (1,)), ((), ())), preferred_element_type=jnp.float32
    )
    grad_normed = lax.psum_scatter(
        grad_part.astype(jnp.bfloat16), "tp", scatter_dimension=1, tiled=True
    ).astype(jnp.float32)
    row_dot = lax.psum(part_dots, "tp")
    own_inputs = lax.dynamic_slice_in_dim(inputs, own_start, own_width, 1)
    own_gain = lax.dynamic_slice_in_dim(norm_gain, own_start, own_width, 0)
    grad_rows = (
        inv_rms * own_gain * grad_normed - own_inputs * (inv_rms * inv_rms) * row_dot / features
    )
    bias_grad = lax.psum(jnp.sum(grad_rows, axis=0), ("enc", "llm"))
    visual_grad = grad_rows.astype(jnp.bfloat16).reshape(1, 1, buckets, capacity, own_width)
    return (key_values[None, None], visual_grad, bias_grad)


def solution(mesh):
    return jax.shard_map(
        per_device,
        mesh=mesh,
        in_specs=(
            P("enc", "llm", None, None, None),
            P("enc", "llm", None),
            P(),
            P(),
            P(None, "tp"),
            P("enc", "llm", None, None, "tp"),
        ),
        out_specs=(P("enc", "llm", None, None, "tp"), P("enc", "llm", None, None, "tp"), P("tp")),
        check_vma=False,
    )
```

```python
import functools

import jax
import jax.numpy as jnp
from jax import lax
from jax.experimental import pallas as pl
from jax.experimental.pallas import tpu as pltpu
from jax.sharding import PartitionSpec as P

RING = 4
LANES = 128
UNIT = 256


def remote(src, dst, send, recv, **where):
    return pltpu.make_async_remote_copy(
        src_ref=src,
        dst_ref=dst,
        send_sem=send,
        recv_sem=recv,
        device_id=where,
        device_id_type=pl.DeviceIdType.MESH,
    )


def kernel(
    counts, bias, gain, vis_hbm, w_hbm, cot_hbm,
    kv_out, vg_out, bg_out,
    vis, w, cot_own, cot_in, xs, xn, inv, proj, kv_own, masked, coef,
    s1, r1, acc, s2, r2, s3, r3, vg,
    p_own, p_in, q_own, q_in, z_own, z_in, f_own, f_in,
    cot_s, cot_r, kv_s, kv_r, z_s, z_r, p_s, p_r, q_s, q_r, f_s, f_r,
    s1_s, s1_r, s2_s, s2_r, s3_s, s3_r, loc,
):
    n_enc, n_llm = lax.axis_size("enc"), lax.axis_size("llm")
    n_tp = lax.axis_size("tp")
    me, group, rank = lax.axis_index("enc"), lax.axis_index("llm"), lax.axis_index("tp")
    chip, core = rank // 2, rank % 2
    units = w.shape[0]
    per_rank = units // n_tp
    features = units * UNIT
    rows = n_enc * 4
    pairs = n_enc // 2

    barrier = pltpu.get_barrier_semaphore()

    def far(i):
        step = (i + 1) // 2
        return lax.rem(me + n_enc // 2 + step * (1 - 2 * lax.rem(i, 2)), n_enc)

    @pl.loop(0, n_enc - 1)
    def _(i):
        pl.semaphore_signal(barrier, 1, device_id={"enc": far(i)})

    for d in range(1, n_llm):
        pl.semaphore_signal(barrier, 1, device_id={"llm": lax.rem(group + d, n_llm)})
    for d in range(1, n_tp):
        pl.semaphore_signal(barrier, 1, device_id={"tp": lax.rem(rank + d, n_tp)})

    get_vis = pltpu.make_async_copy(vis_hbm.at[0, 0], vis, loc.at[0])
    get_w = pltpu.make_async_copy(w_hbm, w, loc.at[1])
    get_cot = pltpu.make_async_copy(cot_hbm.at[0, 0], cot_own, loc.at[2])
    get_vis.start()
    get_w.start()
    get_cot.start()

    get_vis.wait()

    @pl.loop(0, pairs // 2)
    def _(g):
        for h in range(2):
            i = g * 2 + h
            squares = jnp.zeros((8, UNIT), jnp.float32)
            for u in range(units):
                cols = slice(u * UNIT, (u + 1) * UNIT)
                add = bias[:, cols]
                xs[u, i, 0:4, :] = vis[2 * i, :, cols].astype(jnp.float32) + add
                xs[u, i, 4:8, :] = vis[2 * i + 1, :, cols].astype(jnp.float32) + add
                x = xs[u, i]
                squares = squares + x * x
            mean = jnp.sum(squares, axis=1, keepdims=True) * (1.0 / features)
            inv[i] = jnp.broadcast_to(lax.rsqrt(mean + 1e-06), (8, LANES))
        scale = inv[pl.ds(2 * g, 2)].reshape(16, LANES)[:, :1]
        for u in range(units):
            x = xs[u, pl.ds(2 * g, 2)].reshape(16, UNIT)
            xn[u, g] = (x * scale * gain[u]).astype(jnp.bfloat16)

    get_w.wait()
    proj[...] = jnp.zeros_like(proj)

    @pl.loop(0, units)
    def _(u):
        proj[...] += jnp.dot(
            xn[u].reshape(rows, UNIT), w[u], preferred_element_type=jnp.float32
        ).reshape(proj.shape)

    slot = lax.broadcasted_iota(jnp.int32, (4, UNIT), 0)

    @pl.loop(0, pairs)
    def _(i):
        for h in range(2):
            rows4 = proj[i, 4 * h : 4 * h + 4, :]
            kept = jnp.where(slot < counts[0, 0, 2 * i + h], rows4, 0.0)
            kv_own[2 * i + h] = kept.astype(jnp.bfloat16)

    get_cot.wait()
    pl.semaphore_wait(barrier, n_enc - 1 + n_llm - 1 + n_tp - 1)

    def cot_copy(other, at):
        return remote(
            cot_own.at[other], cot_in.at[at], cot_s.at[other], cot_r.at[at], enc=other
        )

    @pl.loop(0, n_enc - 1)
    def _(i):
        cot_copy(far(i), me).start()

    cot_in[me] = cot_own[me]

    @pl.loop(0, n_enc - 1)
    def _(i):
        other = lax.rem(me + 1 + i, n_enc)
        cot_copy(other, other).wait_recv()

    def kv_copy(other, at):
        return remote(
            kv_own.at[other], kv_out.at[0, 0, at], kv_s.at[other], kv_r.at[at], enc=other
        )

    @pl.loop(0, n_enc - 1)
    def _(i):
        kv_copy(far(i), me).start()

    kv_self = pltpu.make_async_copy(kv_own.at[me], kv_out.at[0, 0, me], loc.at[3])
    kv_self.start()

    @pl.loop(0, pairs)
    def _(i):
        for h in range(2):
            got = cot_in[2 * i + h].astype(jnp.float32)
            masked[i, 4 * h : 4 * h + 4, :] = jnp.where(slot < counts[0, 0, 2 * i + h], got, 0.0)
        dots = jnp.sum(masked[i] * proj[i], axis=1, keepdims=True)
        coef[i] = inv[i] * inv[i] * jnp.broadcast_to(dots, (8, LANES)) * (1.0 / features)

    def term(u):
        cot16 = masked[...].reshape(rows, UNIT).astype(jnp.bfloat16)
        grad = lax.dot_general(
            cot16, w[u], (((1,), (1,)), ((), ())), preferred_element_type=jnp.float32
        )
        a = inv[...].reshape(rows, LANES)[:, :1]
        b = coef[...].reshape(rows, LANES)[:, :1]
        return a * gain[u] * grad - xs[u].reshape(rows, UNIT) * b

    def column_sums(j, v, part):
        total = jnp.sum(part, axis=0, keepdims=True)
        for k in range(UNIT // LANES):
            p_own[j, pl.ds(v * (UNIT // LANES) + k, 1), :] = total[:, k * LANES : (k + 1) * LANES]

    def s1_copy(k):
        return remote(s1.at[k], r1.at[k], s1_s.at[k], s1_r.at[k], tp=rank + 1 - 2 * core)

    order = (2, 1, 3, 0)
    for k in order:
        j = lax.rem(chip + k, RING) * 2 + 1 - core
        for v in range(per_rank):
            part = term(j * per_rank + v)
            s1[k, v] = part.astype(jnp.bfloat16)
            column_sums(j, v, part)
        s1_copy(k).start()
    for k in order:
        j = lax.rem(chip + k, RING) * 2 + core
        for v in range(per_rank):
            part = term(j * per_rank + v)
            acc[k, v] = part
            column_sums(j, v, part)

    def p_copy(other, at):
        return remote(p_own.at[other], p_in.at[at], p_s.at[other], p_r.at[at], tp=other)

    for d in range(1, n_tp):
        p_copy(lax.rem(rank + d, n_tp), rank).start()
    p_in[rank] = p_own[rank]

    half = rows // 2

    def pair(k):
        s1_copy(k).wait_recv()
        for v in range(per_rank):
            acc[k, v] += r1[k, v].astype(jnp.float32)

    up = lax.rem(chip + 1, RING) * 2 + core
    down = lax.rem(chip + RING - 1, RING) * 2 + core

    def s2_copy(h):
        return remote(s2.at[h], r2.at[h], s2_s.at[h], s2_r.at[h], tp=(up, down)[h])

    def s3_copy(side, h):
        return remote(
            s3.at[side, h], r3.at[side, h], s3_s.at[side, h], s3_r.at[side, h], tp=(up, down)[side]
        )

    def fill(dst, k, h):
        for v in range(per_rank):
            dst[v] = acc[k, v, h * half : (h + 1) * half, :].astype(jnp.bfloat16)

    pair(2)
    for h in range(2):
        fill(s2.at[h], 2, h)
        s2_copy(h).start()
    for side, k in ((0, 1), (1, 3)):
        pair(k)
        fill(s3.at[side, 1 - side], k, 1 - side)
        s3_copy(side, 1 - side).start()

    for d in range(1, n_tp):
        other = lax.rem(rank + d, n_tp)
        p_copy(other, other).wait_recv()
    q = p_in[0]
    for t in range(1, n_tp):
        q = q + p_in[t]
    q_rows = 8 // n_llm
    for g in range(n_llm):
        q_own[g] = q[g * q_rows : (g + 1) * q_rows, :]

    def q_copy(other, at):
        return remote(q_own.at[other], q_in.at[at], q_s.at[other], q_r.at[at], llm=other)

    for d in range(1, n_llm):
        q_copy(lax.rem(group + d, n_llm), group).start()
    q_in[group] = q_own[group]

    pair(0)
    for side, k in ((0, 1), (1, 3)):
        s2_copy(side).wait_recv()
        for v in range(per_rank):
            acc[k, v, side * half : (side + 1) * half, :] += r2[side, v].astype(jnp.float32)
        fill(s3.at[side, side], k, side)
        s3_copy(side, side).start()

    for d in range(1, n_llm):
        other = lax.rem(group + d, n_llm)
        q_copy(other, other).wait_recv()
    q = q_in[0]
    for g in range(1, n_llm):
        q = q + q_in[g]
    z_own[...] = q

    def z_copy(other, at):
        return remote(z_own, z_in.at[at], z_s.at[other], z_r.at[at], enc=other)

    @pl.loop(0, n_enc - 1)
    def _(i):
        z_copy(far(i), me).start()

    z_in[me] = q

    for h in range(2):
        for side in range(2):
            s3_copy(side, h).wait_recv()
        for v in range(per_rank):
            total = acc[0, v, h * half : (h + 1) * half, :] + (
                r3[0, h, v].astype(jnp.float32) + r3[1, h, v].astype(jnp.float32)
            )
            acc[0, v, h * half : (h + 1) * half, :] = total
    for b in range(n_enc):
        for v in range(per_rank):
            vg[b, :, v * UNIT : (v + 1) * UNIT] = acc[0, v, 4 * b : 4 * b + 4, :].astype(jnp.bfloat16)
    put_vg = pltpu.make_async_copy(vg, vg_out.at[0, 0], loc.at[4])
    put_vg.start()

    @pl.loop(0, n_enc - 1)
    def _(i):
        other = lax.rem(me + 1 + i, n_enc)
        z_copy(other, other).wait_recv()

    q = z_in[0]
    for s in range(1, n_enc):
        q = q + z_in[s]
    f_own[...] = q

    def f_copy(other, at):
        return remote(f_own, f_in.at[at], f_s.at[other], f_r.at[at], llm=other)

    for d in range(1, n_llm):
        f_copy(lax.rem(group + d, n_llm), group).start()
    f_in[group] = q

    put_vg.wait()
    kv_self.wait()

    @pl.loop(0, n_enc - 1)
    def _(i):
        other = lax.rem(me + 1 + i, n_enc)
        kv_copy(other, other).wait_recv()
        kv_copy(other, me).wait_send()
        cot_copy(other, me).wait_send()
        z_copy(other, me).wait_send()

    for d in range(1, n_tp):
        p_copy(lax.rem(rank + d, n_tp), rank).wait_send()
    for k in range(RING):
        s1_copy(k).wait_send()
    for side in range(2):
        s2_copy(side).wait_send()
        for h in range(2):
            s3_copy(side, h).wait_send()
    for d in range(1, n_llm):
        other = lax.rem(group + d, n_llm)
        q_copy(other, group).wait_send()
        f_copy(other, group).wait_send()
        f_copy(other, other).wait_recv()
    for g in range(n_llm):
        bg_out[g * q_rows : (g + 1) * q_rows, :] = f_in[g]


def per_device(visual, counts, merger_bias, norm_gain, kv_weight, kv_cotangent):
    n_enc, cap, features = visual.shape[2:]
    columns = kv_weight.shape[1]
    n_llm, n_tp = lax.axis_size("llm"), lax.axis_size("tp")
    units = features // UNIT
    per_rank = units // n_tp
    rows = n_enc * cap
    own = features // n_tp
    q_rows = 8 // n_llm
    f32, bf16 = jnp.float32, jnp.bfloat16
    vmem, dma = pltpu.VMEM, pltpu.SemaphoreType.DMA
    any_space = pl.BlockSpec(memory_space=pl.ANY)
    in_vmem = pl.BlockSpec(memory_space=pltpu.VMEM)
    scratch = [
        vmem((n_enc, cap, features), bf16),
        vmem((units, UNIT, columns), bf16),
        vmem((n_enc, cap, columns), bf16),
        vmem((n_enc, cap, columns), bf16),
        vmem((units, rows // 8, 8, UNIT), f32),
        vmem((units, rows // 16, 16, UNIT), bf16),
        vmem((rows // 8, 8, LANES), f32),
        vmem((rows // 8, 8, columns), f32),
        vmem((n_enc, cap, columns), bf16),
        vmem((rows // 8, 8, columns), f32),
        vmem((rows // 8, 8, LANES), f32),
        vmem((RING, per_rank, rows, UNIT), bf16),
        vmem((RING, per_rank, rows, UNIT), bf16),
        vmem((RING, per_rank, rows, UNIT), f32),
        vmem((2, per_rank, rows // 2, UNIT), bf16),
        vmem((2, per_rank, rows // 2, UNIT), bf16),
        vmem((2, 2, per_rank, rows // 2, UNIT), bf16),
        vmem((2, 2, per_rank, rows // 2, UNIT), bf16),
        vmem((n_enc, cap, own), bf16),
        vmem((n_tp, 8, LANES), f32),
        vmem((n_tp, 8, LANES), f32),
        vmem((n_llm, q_rows, LANES), f32),
        vmem((n_llm, q_rows, LANES), f32),
        vmem((q_rows, LANES), f32),
        vmem((n_enc, q_rows, LANES), f32),
        vmem((q_rows, LANES), f32),
        vmem((n_llm, q_rows, LANES), f32),
        *[dma((n_enc,))] * 6,
        *[dma((n_tp,))] * 2,
        *[dma((n_llm,))] * 4,
        *[dma((RING,))] * 2,
        *[dma((2,))] * 2,
        *[dma((2, 2))] * 2,
        dma((5,)),
    ]
    key_values, visual_grad, bias_grad = pl.pallas_call(
        kernel,
        out_shape=(
            jax.ShapeDtypeStruct((1, 1, n_enc, cap, columns), bf16),
            jax.ShapeDtypeStruct((1, 1, n_enc, cap, own), bf16),
            jax.ShapeDtypeStruct((8, LANES), f32),
        ),
        in_specs=[
            pl.BlockSpec(memory_space=pltpu.SMEM),
            in_vmem,
            in_vmem,
            any_space,
            any_space,
            any_space,
        ],
        out_specs=(any_space, any_space, in_vmem),
        scratch_shapes=scratch,
        compiler_params=pltpu.CompilerParams(
            collective_id=0, has_side_effects=True, vmem_limit_bytes=48 << 20
        ),
    )(
        counts,
        merger_bias.reshape(1, features),
        norm_gain.reshape(units, 1, UNIT),
        visual,
        kv_weight.reshape(units, UNIT, columns),
        kv_cotangent,
    )
    return (key_values, visual_grad, bias_grad.reshape(own))


def solution(mesh):
    return jax.shard_map(
        per_device,
        mesh=mesh,
        in_specs=(
            P("enc", "llm", None, None, None),
            P("enc", "llm", None),
            P(),
            P(),
            P(None, "tp"),
            P("enc", "llm", None, None, "tp"),
        ),
        out_specs=(P("enc", "llm", None, None, "tp"), P("enc", "llm", None, None, "tp"), P("tp")),
        check_vma=False,
    )
```

```python
import functools

import jax
import jax.numpy as jnp
from jax import lax
from jax.experimental import pallas as pl
from jax.experimental.pallas import tpu as pltpu
from jax.sharding import PartitionSpec as P

RING = 4
LANES = 128
UNIT = 256


def remote(src, dst, send, recv, **where):
    return pltpu.make_async_remote_copy(
        src_ref=src,
        dst_ref=dst,
        send_sem=send,
        recv_sem=recv,
        device_id=where,
        device_id_type=pl.DeviceIdType.MESH,
    )


def kernel(
    counts_hbm, bias_hbm, gain_hbm, vis_hbm, w_hbm, cot_hbm,
    kv_out, vg_out, bg_out,
    counts, bias, gain, vis, w, cot_own, cot_in, hop, xs, xn, inv, proj, kv_own, masked, coef,
    s1, r1, acc, s2, r2, s3, r3, vg,
    p_own, p_in, q_own, q_in, z_own, z_in, f_own, f_in,
    cot_s, cot_r, kv_s, kv_r, z_s, z_r, p_s, p_r, q_s, q_r, f_s, f_r,
    s1_s, s1_r, s2_s, s2_r, s3_s, s3_r, hop_s, hop_r, loc,
):
    n_enc, n_llm = lax.axis_size("enc"), lax.axis_size("llm")
    n_tp = lax.axis_size("tp")
    me, group, rank = lax.axis_index("enc"), lax.axis_index("llm"), lax.axis_index("tp")
    chip, core = rank // 2, rank % 2
    units = w.shape[0]
    per_rank = units // n_tp
    features = units * UNIT
    rows = n_enc * 4
    pairs = n_enc // 2

    reach = n_enc // 4

    def at_step(d):
        return lax.rem(me + d + n_enc, n_enc)

    barrier = pltpu.get_barrier_semaphore()

    @pl.loop(0, reach)
    def _(i):
        d = reach - i
        pl.semaphore_signal(barrier, 1, device_id={"enc": at_step(d)})
        pl.semaphore_signal(barrier, 1, device_id={"enc": at_step(-d)})

    for d in range(1, n_llm):
        pl.semaphore_signal(barrier, 1, device_id={"llm": lax.rem(group + d, n_llm)})
    for d in range(1, n_tp):
        pl.semaphore_signal(barrier, 1, device_id={"tp": lax.rem(rank + d, n_tp)})

    loads = [
        pltpu.make_async_copy(src, dst, loc.at[i])
        for i, (src, dst) in enumerate(
            (
                (vis_hbm.at[0, 0], vis),
                (bias_hbm, bias),
                (gain_hbm, gain),
                (cot_hbm.at[0, 0], cot_own),
                (counts_hbm, counts),
                (w_hbm, w),
            )
        )
    ]
    for load in loads:
        load.start()

    for load in loads[:3]:
        load.wait()

    @pl.loop(0, pairs // 2)
    def _(g):
        for h in range(2):
            i = g * 2 + h
            squares = jnp.zeros((8, UNIT), jnp.float32)
            for u in range(units):
                cols = slice(u * UNIT, (u + 1) * UNIT)
                add = bias[:, cols]
                xs[u, i, 0:4, :] = vis[2 * i, :, cols].astype(jnp.float32) + add
                xs[u, i, 4:8, :] = vis[2 * i + 1, :, cols].astype(jnp.float32) + add
                x = xs[u, i]
                squares = squares + x * x
            mean = jnp.sum(squares, axis=1, keepdims=True) * (1.0 / features)
            inv[i] = jnp.broadcast_to(lax.rsqrt(mean + 1e-06), (8, LANES))
        scale = inv[pl.ds(2 * g, 2)].reshape(16, LANES)[:, :1]
        for u in range(units):
            x = xs[u, pl.ds(2 * g, 2)].reshape(16, UNIT)
            xn[u, g] = (x * scale * gain[u]).astype(jnp.bfloat16)

    for load in loads[3:5]:
        load.wait()
    pl.semaphore_wait(barrier, 2 * reach + n_llm - 1 + n_tp - 1)

    def cot_copy(to, at):
        return remote(cot_own.at[to], cot_in.at[at], cot_s.at[to], cot_r.at[at], enc=to)

    def away(side, d):
        return at_step(d - 2 * side * d)

    def out_copy(side, q):
        to = away(side, reach + q)
        return remote(
            cot_own.at[to], hop.at[side, q - 1], cot_s.at[to], hop_r.at[side, q - 1],
            enc=away(side, reach),
        )

    def on_copy(side, q):
        origin = away(side, -reach)
        return remote(
            hop.at[side, q - 1], cot_in.at[origin], hop_s.at[side, q - 1], cot_r.at[origin],
            enc=away(side, q),
        )

    @pl.loop(0, reach)
    def _(i):
        out_copy(0, reach - i).start()

        @pl.when(i > 0)
        def _():
            out_copy(1, reach - i).start()

    @pl.loop(0, reach)
    def _(i):
        for side in range(2):
            cot_copy(away(side, reach - i), me).start()

    cot_in[me] = cot_own[me]

    loads[5].wait()
    proj[...] = jnp.zeros_like(proj)
    step_units = 4

    @pl.loop(0, units // step_units)
    def _(t):
        total = jnp.zeros((rows, UNIT), jnp.float32)
        for k in range(step_units):
            u = t * step_units + k
            total = total + jnp.dot(
                xn[u].reshape(rows, UNIT), w[u], preferred_element_type=jnp.float32
            )
        proj[...] += total.reshape(proj.shape)

    slot = lax.broadcasted_iota(jnp.int32, (4, UNIT), 0)

    @pl.loop(0, pairs)
    def _(i):
        for h in range(2):
            rows4 = proj[i, 4 * h : 4 * h + 4, :]
            kept = jnp.where(slot < counts[0, 0, 2 * i + h], rows4, 0.0)
            kv_own[2 * i + h] = kept.astype(jnp.bfloat16)

    def kv_copy(to, at):
        return remote(kv_own.at[to], kv_out.at[0, 0, at], kv_s.at[to], kv_r.at[at], enc=to)

    @pl.loop(0, reach)
    def _(i):
        for side in range(2):
            kv_copy(away(side, reach - i), me).start()

    kv_self = pltpu.make_async_copy(kv_own.at[me], kv_out.at[0, 0, me], loc.at[6])
    kv_self.start()

    @pl.loop(0, reach)
    def _(i):
        out_copy(0, reach - i).wait_recv()
        on_copy(0, reach - i).start()

        @pl.when(i > 0)
        def _():
            out_copy(1, reach - i).wait_recv()
            on_copy(1, reach - i).start()

    @pl.loop(0, pairs)
    def _(n):
        step = (n + 1) // 2
        i = lax.rem(me // 2 + step * (1 - 2 * lax.rem(n, 2)) + pairs, pairs)
        for h in range(2):
            other = 2 * i + h

            @pl.when(other != me)
            def _():
                cot_copy(other, other).wait_recv()

        for h in range(2):
            got = cot_in[2 * i + h].astype(jnp.float32)
            masked[i, 4 * h : 4 * h + 4, :] = jnp.where(slot < counts[0, 0, 2 * i + h], got, 0.0)
        dots = jnp.sum(masked[i] * proj[i], axis=1, keepdims=True)
        coef[i] = inv[i] * inv[i] * jnp.broadcast_to(dots, (8, LANES)) * (1.0 / features)

    def term(u):
        cot16 = masked[...].reshape(rows, UNIT).astype(jnp.bfloat16)
        grad = lax.dot_general(
            cot16, w[u], (((1,), (1,)), ((), ())), preferred_element_type=jnp.float32
        )
        a = inv[...].reshape(rows, LANES)[:, :1]
        b = coef[...].reshape(rows, LANES)[:, :1]
        return a * gain[u] * grad - xs[u].reshape(rows, UNIT) * b

    def column_sums(j, v, part):
        total = jnp.sum(part, axis=0, keepdims=True)
        for k in range(UNIT // LANES):
            p_own[j, pl.ds(v * (UNIT // LANES) + k, 1), :] = total[:, k * LANES : (k + 1) * LANES]

    def s1_copy(k):
        return remote(s1.at[k], r1.at[k], s1_s.at[k], s1_r.at[k], tp=rank + 1 - 2 * core)

    order = (2, 1, 3, 0)
    for k in order:
        j = lax.rem(chip + k, RING) * 2 + 1 - core
        for v in range(per_rank):
            part = term(j * per_rank + v)
            s1[k, v] = part.astype(jnp.bfloat16)
            column_sums(j, v, part)
    for k in order:
        j = lax.rem(chip + k, RING) * 2 + core
        for v in range(per_rank):
            part = term(j * per_rank + v)
            acc[k, v] = part
            column_sums(j, v, part)

    def p_copy(other, at):
        return remote(p_own.at[other], p_in.at[at], p_s.at[other], p_r.at[at], tp=other)

    for d in range(1, n_tp):
        p_copy(lax.rem(rank + d, n_tp), rank).start()
    p_in[rank] = p_own[rank]
    for k in order:
        s1_copy(k).start()

    @pl.loop(reach + 1, n_enc // 2)
    def _(d):
        for side in range(2):
            kv_copy(away(side, d), me).start()

    kv_copy(at_step(n_enc // 2), me).start()

    half = rows // 2

    def pair(k):
        s1_copy(k).wait_recv()
        for v in range(per_rank):
            acc[k, v] += r1[k, v].astype(jnp.float32)

    up = lax.rem(chip + 1, RING) * 2 + core
    down = lax.rem(chip + RING - 1, RING) * 2 + core

    def s2_copy(h):
        return remote(s2.at[h], r2.at[h], s2_s.at[h], s2_r.at[h], tp=(up, down)[h])

    def s3_copy(side, h):
        return remote(
            s3.at[side, h], r3.at[side, h], s3_s.at[side, h], s3_r.at[side, h], tp=(up, down)[side]
        )

    def fill(dst, k, h):
        for v in range(per_rank):
            dst[v] = acc[k, v, h * half : (h + 1) * half, :].astype(jnp.bfloat16)

    pair(2)
    for h in range(2):
        fill(s2.at[h], 2, h)
        s2_copy(h).start()
    for side, k in ((0, 1), (1, 3)):
        pair(k)
        fill(s3.at[side, 1 - side], k, 1 - side)
        s3_copy(side, 1 - side).start()

    for d in range(1, n_tp):
        other = lax.rem(rank + d, n_tp)
        p_copy(other, other).wait_recv()
    q = p_in[0]
    for t in range(1, n_tp):
        q = q + p_in[t]
    q_rows = 8 // n_llm
    for g in range(n_llm):
        q_own[g] = q[g * q_rows : (g + 1) * q_rows, :]

    def q_copy(other, at):
        return remote(q_own.at[other], q_in.at[at], q_s.at[other], q_r.at[at], llm=other)

    for d in range(1, n_llm):
        q_copy(lax.rem(group + d, n_llm), group).start()
    q_in[group] = q_own[group]

    pair(0)

    for d in range(1, n_llm):
        other = lax.rem(group + d, n_llm)
        q_copy(other, other).wait_recv()
    q = q_in[0]
    for g in range(1, n_llm):
        q = q + q_in[g]
    z_own[...] = q

    def z_copy(other, at):
        return remote(z_own, z_in.at[at], z_s.at[other], z_r.at[at], enc=other)

    @pl.loop(0, n_enc - 1)
    def _(i):
        step = (i + 1) // 2
        z_copy(lax.rem(me + n_enc // 2 + step * (1 - 2 * lax.rem(i, 2)), n_enc), me).start()

    z_in[me] = q

    for side, k in ((0, 1), (1, 3)):
        s2_copy(side).wait_recv()
        for v in range(per_rank):
            acc[k, v, side * half : (side + 1) * half, :] += r2[side, v].astype(jnp.float32)
        fill(s3.at[side, side], k, side)
        s3_copy(side, side).start()

    for h in range(2):
        for side in range(2):
            s3_copy(side, h).wait_recv()
        for v in range(per_rank):
            total = acc[0, v, h * half : (h + 1) * half, :] + (
                r3[0, h, v].astype(jnp.float32) + r3[1, h, v].astype(jnp.float32)
            )
            acc[0, v, h * half : (h + 1) * half, :] = total
    for b in range(n_enc):
        for v in range(per_rank):
            vg[b, :, v * UNIT : (v + 1) * UNIT] = acc[0, v, 4 * b : 4 * b + 4, :].astype(jnp.bfloat16)
    put_vg = pltpu.make_async_copy(vg, vg_out.at[0, 0], loc.at[7])
    put_vg.start()

    @pl.loop(0, n_enc - 1)
    def _(i):
        other = lax.rem(me + 1 + i, n_enc)
        z_copy(other, other).wait_recv()

    q = z_in[0]
    for s in range(1, n_enc):
        q = q + z_in[s]
    f_own[...] = q

    def f_copy(other, at):
        return remote(f_own, f_in.at[at], f_s.at[other], f_r.at[at], llm=other)

    for d in range(1, n_llm):
        f_copy(lax.rem(group + d, n_llm), group).start()
    f_in[group] = q

    put_vg.wait()
    kv_self.wait()

    @pl.loop(0, n_enc - 1)
    def _(i):
        other = lax.rem(me + 1 + i, n_enc)
        kv_copy(other, other).wait_recv()
        kv_copy(other, me).wait_send()
        cot_copy(other, me).wait_send()
        z_copy(other, me).wait_send()

    @pl.loop(0, reach)
    def _(i):
        on_copy(0, reach - i).wait_send()

        @pl.when(i > 0)
        def _():
            on_copy(1, reach - i).wait_send()

    for d in range(1, n_tp):
        p_copy(lax.rem(rank + d, n_tp), rank).wait_send()
    for k in range(RING):
        s1_copy(k).wait_send()
    for side in range(2):
        s2_copy(side).wait_send()
        for h in range(2):
            s3_copy(side, h).wait_send()
    for d in range(1, n_llm):
        other = lax.rem(group + d, n_llm)
        q_copy(other, group).wait_send()
        f_copy(other, group).wait_send()
        f_copy(other, other).wait_recv()
    for g in range(n_llm):
        bg_out[g * q_rows : (g + 1) * q_rows, :] = f_in[g]


def per_device(visual, counts, merger_bias, norm_gain, kv_weight, kv_cotangent):
    n_enc, cap, features = visual.shape[2:]
    columns = kv_weight.shape[1]
    n_llm, n_tp = lax.axis_size("llm"), lax.axis_size("tp")
    units = features // UNIT
    per_rank = units // n_tp
    rows = n_enc * cap
    own = features // n_tp
    q_rows = 8 // n_llm
    f32, bf16 = jnp.float32, jnp.bfloat16
    vmem, dma = pltpu.VMEM, pltpu.SemaphoreType.DMA
    any_space = pl.BlockSpec(memory_space=pl.ANY)
    in_hbm = any_space
    reach = n_enc // 4
    in_vmem = pl.BlockSpec(memory_space=pltpu.VMEM)
    scratch = [
        pltpu.SMEM((1, 1, n_enc), jnp.int32),
        vmem((1, features), f32),
        vmem((units, 1, UNIT), f32),
        vmem((n_enc, cap, features), bf16),
        vmem((units, UNIT, columns), bf16),
        vmem((n_enc, cap, columns), bf16),
        vmem((n_enc, cap, columns), bf16),
        vmem((2, reach, cap, columns), bf16),
        vmem((units, rows // 8, 8, UNIT), f32),
        vmem((units, rows // 16, 16, UNIT), bf16),
        vmem((rows // 8, 8, LANES), f32),
        vmem((rows // 8, 8, columns), f32),
        vmem((n_enc, cap, columns), bf16),
        vmem((rows // 8, 8, columns), f32),
        vmem((rows // 8, 8, LANES), f32),
        vmem((RING, per_rank, rows, UNIT), bf16),
        vmem((RING, per_rank, rows, UNIT), bf16),
        vmem((RING, per_rank, rows, UNIT), f32),
        vmem((2, per_rank, rows // 2, UNIT), bf16),
        vmem((2, per_rank, rows // 2, UNIT), bf16),
        vmem((2, 2, per_rank, rows // 2, UNIT), bf16),
        vmem((2, 2, per_rank, rows // 2, UNIT), bf16),
        vmem((n_enc, cap, own), bf16),
        vmem((n_tp, 8, LANES), f32),
        vmem((n_tp, 8, LANES), f32),
        vmem((n_llm, q_rows, LANES), f32),
        vmem((n_llm, q_rows, LANES), f32),
        vmem((q_rows, LANES), f32),
        vmem((n_enc, q_rows, LANES), f32),
        vmem((q_rows, LANES), f32),
        vmem((n_llm, q_rows, LANES), f32),
        *[dma((n_enc,))] * 6,
        *[dma((n_tp,))] * 2,
        *[dma((n_llm,))] * 4,
        *[dma((RING,))] * 2,
        *[dma((2,))] * 2,
        *[dma((2, 2))] * 2,
        *[dma((2, reach))] * 2,
        dma((8,)),
    ]
    key_values, visual_grad, bias_grad = pl.pallas_call(
        kernel,
        out_shape=(
            jax.ShapeDtypeStruct((1, 1, n_enc, cap, columns), bf16),
            jax.ShapeDtypeStruct((1, 1, n_enc, cap, own), bf16),
            jax.ShapeDtypeStruct((8, LANES), f32),
        ),
        in_specs=[in_hbm] * 6,
        out_specs=(any_space, any_space, in_vmem),
        scratch_shapes=scratch,
        compiler_params=pltpu.CompilerParams(
            collective_id=0, has_side_effects=True, vmem_limit_bytes=67043328
        ),
    )(
        counts,
        merger_bias.reshape(1, features),
        norm_gain.reshape(units, 1, UNIT),
        visual,
        kv_weight.reshape(units, UNIT, columns),
        kv_cotangent,
    )
    return (key_values, visual_grad, bias_grad.reshape(own))


def solution(mesh):
    return jax.shard_map(
        per_device,
        mesh=mesh,
        in_specs=(
            P("enc", "llm", None, None, None),
            P("enc", "llm", None),
            P(),
            P(),
            P(None, "tp"),
            P("enc", "llm", None, None, "tp"),
        ),
        out_specs=(P("enc", "llm", None, None, "tp"), P("enc", "llm", None, None, "tp"), P("tp")),
        check_vma=False,
    )
```

```python
import functools

import jax
import jax.numpy as jnp
from jax import lax
from jax.experimental import pallas as pl
from jax.experimental.pallas import tpu as pltpu
from jax.sharding import PartitionSpec as P

RING = 4
LANES = 128
UNIT = 256


def remote(src, dst, send, recv, **where):
    return pltpu.make_async_remote_copy(
        src_ref=src,
        dst_ref=dst,
        send_sem=send,
        recv_sem=recv,
        device_id=where,
        device_id_type=pl.DeviceIdType.MESH,
    )


def kernel(
    counts_hbm, bias_hbm, gain_hbm, vis_hbm, w_hbm, cot_hbm,
    kv_out, vg_out, bg_out,
    counts, bias, gain, vis, w, cot_own, cot_in, hop, xs, xn, inv, proj, kv_own, masked, coef,
    s1, r1, acc, s2, r2, s3, r3, vg,
    p_own, p_in, z_own, z_in, f_own, kv_hop,
    cot_s, cot_r, kv_s, kv_r, z_s, z_r, p_s, p_r, f_s, f_r, kv_hop_s, kv_hop_r,
    s1_s, s1_r, s2_s, s2_r, s3_s, s3_r, hop_s, hop_r, loc,
):
    n_enc, n_llm = lax.axis_size("enc"), lax.axis_size("llm")
    n_tp = lax.axis_size("tp")
    me, group, rank = lax.axis_index("enc"), lax.axis_index("llm"), lax.axis_index("tp")
    chip, core = rank // 2, rank % 2
    units = w.shape[0]
    per_rank = units // n_tp
    features = units * UNIT
    rows = n_enc * 4
    pairs = n_enc // 2

    reach = n_enc // 4

    def at_step(d):
        return lax.rem(me + d + n_enc, n_enc)

    barrier = pltpu.get_barrier_semaphore()

    @pl.loop(0, reach)
    def _(i):
        d = reach - i
        pl.semaphore_signal(barrier, 1, device_id={"enc": at_step(d)})
        pl.semaphore_signal(barrier, 1, device_id={"enc": at_step(-d)})

    plane = n_llm * n_tp
    q_rows = 8 // n_llm

    def in_plane(i):
        place = lax.rem(group * n_tp + rank + 1 + i, plane)
        return place // n_tp, lax.rem(place, n_tp)

    @pl.loop(0, plane - 1)
    def _(i):
        g, t = in_plane(i)
        pl.semaphore_signal(barrier, 1, device_id={"llm": g, "tp": t})

    loads = [
        pltpu.make_async_copy(src, dst, loc.at[i])
        for i, (src, dst) in enumerate(
            (
                (vis_hbm.at[0, 0], vis),
                (bias_hbm, bias),
                (gain_hbm, gain),
                (cot_hbm.at[0, 0], cot_own),
                (counts_hbm, counts),
                (w_hbm, w),
            )
        )
    ]
    for load in loads:
        load.start()

    for load in loads[:3]:
        load.wait()

    @pl.loop(0, pairs // 2)
    def _(g):
        for h in range(2):
            i = g * 2 + h
            squares = jnp.zeros((8, UNIT), jnp.float32)
            for u in range(units):
                cols = slice(u * UNIT, (u + 1) * UNIT)
                add = bias[:, cols]
                xs[u, i, 0:4, :] = vis[2 * i, :, cols].astype(jnp.float32) + add
                xs[u, i, 4:8, :] = vis[2 * i + 1, :, cols].astype(jnp.float32) + add
                x = xs[u, i]
                squares = squares + x * x
            mean = jnp.sum(squares, axis=1, keepdims=True) * (1.0 / features)
            inv[i] = jnp.broadcast_to(lax.rsqrt(mean + 1e-06), (8, LANES))
        scale = inv[pl.ds(2 * g, 2)].reshape(16, LANES)[:, :1]
        for u in range(units):
            x = xs[u, pl.ds(2 * g, 2)].reshape(16, UNIT)
            xn[u, g] = (x * scale * gain[u]).astype(jnp.bfloat16)

    for load in loads[3:5]:
        load.wait()
    pl.semaphore_wait(barrier, 2 * reach + plane - 1)

    def cot_copy(to, at):
        return remote(cot_own.at[to], cot_in.at[at], cot_s.at[to], cot_r.at[at], enc=to)

    def away(side, d):
        return at_step(d - 2 * side * d)

    def out_copy(side, q):
        to = away(side, reach + q)
        return remote(
            cot_own.at[to], hop.at[side, q - 1], cot_s.at[to], hop_r.at[side, q - 1],
            enc=away(side, reach),
        )

    def on_copy(side, q):
        origin = away(side, -reach)
        return remote(
            hop.at[side, q - 1], cot_in.at[origin], hop_s.at[side, q - 1], cot_r.at[origin],
            enc=away(side, q),
        )

    @pl.loop(0, reach)
    def _(i):
        out_copy(0, reach - i).start()

        @pl.when(i > 0)
        def _():
            out_copy(1, reach - i).start()

    @pl.loop(0, reach)
    def _(i):
        for side in range(2):
            cot_copy(away(side, reach - i), me).start()

    cot_in[me] = cot_own[me]

    loads[5].wait()
    proj[...] = jnp.zeros_like(proj)
    step_units = 4

    @pl.loop(0, units // step_units)
    def _(t):
        total = jnp.zeros((rows, UNIT), jnp.float32)
        for k in range(step_units):
            u = t * step_units + k
            total = total + jnp.dot(
                xn[u].reshape(rows, UNIT), w[u], preferred_element_type=jnp.float32
            )
        proj[...] += total.reshape(proj.shape)

    slot = lax.broadcasted_iota(jnp.int32, (4, UNIT), 0)

    @pl.loop(0, pairs)
    def _(i):
        for h in range(2):
            rows4 = proj[i, 4 * h : 4 * h + 4, :]
            kept = jnp.where(slot < counts[0, 0, 2 * i + h], rows4, 0.0)
            kv_own[2 * i + h] = kept.astype(jnp.bfloat16)

    def kv_copy(to, at):
        return remote(kv_own.at[to], kv_out.at[0, 0, at], kv_s.at[to], kv_r.at[at], enc=to)

    def kv_out_copy(side, q):
        to = away(side, reach + q)
        return remote(
            kv_own.at[to], kv_hop.at[side, q - 1], kv_s.at[to], kv_hop_r.at[side, q - 1],
            enc=away(side, reach),
        )

    def kv_on_copy(side, q):
        origin = away(side, -reach)
        return remote(
            kv_hop.at[side, q - 1], kv_out.at[0, 0, origin], kv_hop_s.at[side, q - 1],
            kv_r.at[origin], enc=away(side, q),
        )

    @pl.loop(0, reach)
    def _(i):
        kv_out_copy(0, reach - i).start()

        @pl.when(i > 0)
        def _():
            kv_out_copy(1, reach - i).start()

    @pl.loop(0, reach)
    def _(i):
        for side in range(2):
            kv_copy(away(side, reach - i), me).start()

    kv_self = pltpu.make_async_copy(kv_own.at[me], kv_out.at[0, 0, me], loc.at[6])
    kv_self.start()

    @pl.loop(0, reach)
    def _(i):
        out_copy(0, reach - i).wait_recv()
        on_copy(0, reach - i).start()

        @pl.when(i > 0)
        def _():
            out_copy(1, reach - i).wait_recv()
            on_copy(1, reach - i).start()

    @pl.loop(0, pairs)
    def _(n):
        step = (n + 1) // 2
        i = lax.rem(me // 2 + step * (1 - 2 * lax.rem(n, 2)) + pairs, pairs)
        for h in range(2):
            other = 2 * i + h

            @pl.when(other != me)
            def _():
                cot_copy(other, other).wait_recv()

        for h in range(2):
            got = cot_in[2 * i + h].astype(jnp.float32)
            masked[i, 4 * h : 4 * h + 4, :] = jnp.where(slot < counts[0, 0, 2 * i + h], got, 0.0)
        dots = jnp.sum(masked[i] * proj[i], axis=1, keepdims=True)
        coef[i] = inv[i] * inv[i] * jnp.broadcast_to(dots, (8, LANES)) * (1.0 / features)

    def term(u):
        cot16 = masked[...].reshape(rows, UNIT).astype(jnp.bfloat16)
        grad = lax.dot_general(
            cot16, w[u], (((1,), (1,)), ((), ())), preferred_element_type=jnp.float32
        )
        a = inv[...].reshape(rows, LANES)[:, :1]
        b = coef[...].reshape(rows, LANES)[:, :1]
        return a * gain[u] * grad - xs[u].reshape(rows, UNIT) * b

    def column_sums(j, v, part):
        total = jnp.sum(part, axis=0, keepdims=True)
        for k in range(UNIT // LANES):
            g, r = divmod(v * (UNIT // LANES) + k, q_rows)
            p_own[g, j, r : r + 1, :] = total[:, k * LANES : (k + 1) * LANES]

    def s1_copy(k):
        return remote(s1.at[k], r1.at[k], s1_s.at[k], s1_r.at[k], tp=rank + 1 - 2 * core)

    order = (2, 1, 3, 0)
    for k in order:
        j = lax.rem(chip + k, RING) * 2 + 1 - core
        for v in range(per_rank):
            part = term(j * per_rank + v)
            s1[k, v] = part.astype(jnp.bfloat16)
            column_sums(j, v, part)
    for k in order:
        j = lax.rem(chip + k, RING) * 2 + core
        for v in range(per_rank):
            part = term(j * per_rank + v)
            acc[k, v] = part
            column_sums(j, v, part)

    def p_copy(g, t, at_g, at_t):
        return remote(
            p_own.at[g, t], p_in.at[at_g, at_t], p_s.at[g, t], p_r.at[at_g, at_t], llm=g, tp=t
        )

    @pl.loop(0, plane - 1)
    def _(i):
        p_copy(*in_plane(i), group, rank).start()

    p_in[group, rank] = p_own[group, rank]
    for k in order:
        s1_copy(k).start()

    @pl.loop(0, reach)
    def _(i):
        kv_out_copy(0, reach - i).wait_recv()
        kv_on_copy(0, reach - i).start()

        @pl.when(i > 0)
        def _():
            kv_out_copy(1, reach - i).wait_recv()
            kv_on_copy(1, reach - i).start()

    half = rows // 2

    def pair(k):
        s1_copy(k).wait_recv()
        for v in range(per_rank):
            acc[k, v] += r1[k, v].astype(jnp.float32)

    up = lax.rem(chip + 1, RING) * 2 + core
    down = lax.rem(chip + RING - 1, RING) * 2 + core

    def s2_copy(h):
        return remote(s2.at[h], r2.at[h], s2_s.at[h], s2_r.at[h], tp=(up, down)[h])

    def s3_copy(side, h):
        return remote(
            s3.at[side, h], r3.at[side, h], s3_s.at[side, h], s3_r.at[side, h], tp=(up, down)[side]
        )

    def fill(dst, k, h):
        for v in range(per_rank):
            dst[v] = acc[k, v, h * half : (h + 1) * half, :].astype(jnp.bfloat16)

    pair(2)
    for h in range(2):
        fill(s2.at[h], 2, h)
        s2_copy(h).start()
    for side, k in ((0, 1), (1, 3)):
        pair(k)
        fill(s3.at[side, 1 - side], k, 1 - side)
        s3_copy(side, 1 - side).start()

    pair(0)

    @pl.loop(0, plane - 1)
    def _(i):
        g, t = in_plane(i)
        p_copy(g, t, g, t).wait_recv()

    q = jnp.zeros((q_rows, LANES), jnp.float32)
    for g in range(n_llm):
        for t in range(n_tp):
            q = q + p_in[g, t]
    z_own[...] = q

    def z_copy(other, at):
        return remote(z_own, z_in.at[at], z_s.at[other], z_r.at[at], enc=other)

    @pl.loop(0, n_enc - 1)
    def _(i):
        step = (i + 1) // 2
        z_copy(lax.rem(me + n_enc // 2 + step * (1 - 2 * lax.rem(i, 2)), n_enc), me).start()

    z_in[me] = q

    for side, k in ((0, 1), (1, 3)):
        s2_copy(side).wait_recv()
        for v in range(per_rank):
            acc[k, v, side * half : (side + 1) * half, :] += r2[side, v].astype(jnp.float32)
        fill(s3.at[side, side], k, side)
        s3_copy(side, side).start()

    for h in range(2):
        for side in range(2):
            s3_copy(side, h).wait_recv()
        for v in range(per_rank):
            total = acc[0, v, h * half : (h + 1) * half, :] + (
                r3[0, h, v].astype(jnp.float32) + r3[1, h, v].astype(jnp.float32)
            )
            acc[0, v, h * half : (h + 1) * half, :] = total
    for b in range(n_enc):
        for v in range(per_rank):
            vg[b, :, v * UNIT : (v + 1) * UNIT] = acc[0, v, 4 * b : 4 * b + 4, :].astype(jnp.bfloat16)
    put_vg = pltpu.make_async_copy(vg, vg_out.at[0, 0], loc.at[7])
    put_vg.start()

    @pl.loop(0, n_enc - 1)
    def _(i):
        other = lax.rem(me + 1 + i, n_enc)
        z_copy(other, other).wait_recv()

    q = z_in[0]
    for s in range(1, n_enc):
        q = q + z_in[s]
    f_own[...] = q

    def f_copy(other, at):
        return remote(f_own, bg_out.at[at], f_s.at[other], f_r.at[at], llm=other)

    for d in range(1, n_llm):
        f_copy(lax.rem(group + d, n_llm), group).start()
    put_f = pltpu.make_async_copy(f_own, bg_out.at[group], loc.at[8])
    put_f.start()

    put_vg.wait()
    kv_self.wait()
    put_f.wait()

    @pl.loop(0, n_enc - 1)
    def _(i):
        other = lax.rem(me + 1 + i, n_enc)
        kv_copy(other, other).wait_recv()
        kv_copy(other, me).wait_send()
        cot_copy(other, me).wait_send()
        z_copy(other, me).wait_send()

    @pl.loop(0, reach)
    def _(i):
        on_copy(0, reach - i).wait_send()
        kv_on_copy(0, reach - i).wait_send()

        @pl.when(i > 0)
        def _():
            on_copy(1, reach - i).wait_send()
            kv_on_copy(1, reach - i).wait_send()

    @pl.loop(0, plane - 1)
    def _(i):
        p_copy(*in_plane(i), group, rank).wait_send()

    for k in range(RING):
        s1_copy(k).wait_send()
    for side in range(2):
        s2_copy(side).wait_send()
        for h in range(2):
            s3_copy(side, h).wait_send()
    for d in range(1, n_llm):
        other = lax.rem(group + d, n_llm)
        f_copy(other, group).wait_send()
        f_copy(other, other).wait_recv()


def write_back(kv, vg, bg, kv_out, vg_out, bg_out, sems):
    puts = [
        pltpu.make_async_copy(src, dst, sems.at[i])
        for i, (src, dst) in enumerate(((vg, vg_out), (kv, kv_out), (bg, bg_out)))
    ]
    for put in puts:
        put.start()
    for put in puts:
        put.wait()


def per_device(visual, counts, merger_bias, norm_gain, kv_weight, kv_cotangent):
    n_enc, cap, features = visual.shape[2:]
    columns = kv_weight.shape[1]
    n_llm, n_tp = lax.axis_size("llm"), lax.axis_size("tp")
    units = features // UNIT
    per_rank = units // n_tp
    rows = n_enc * cap
    own = features // n_tp
    q_rows = 8 // n_llm
    f32, bf16 = jnp.float32, jnp.bfloat16
    vmem, dma = pltpu.VMEM, pltpu.SemaphoreType.DMA
    any_space = pl.BlockSpec(memory_space=pl.ANY)
    in_hbm = any_space
    reach = n_enc // 4
    scratch = [
        pltpu.SMEM((1, 1, n_enc), jnp.int32),
        vmem((1, features), f32),
        vmem((units, 1, UNIT), f32),
        vmem((n_enc, cap, features), bf16),
        vmem((units, UNIT, columns), bf16),
        vmem((n_enc, cap, columns), bf16),
        vmem((n_enc, cap, columns), bf16),
        vmem((2, reach, cap, columns), bf16),
        vmem((units, rows // 8, 8, UNIT), f32),
        vmem((units, rows // 16, 16, UNIT), bf16),
        vmem((rows // 8, 8, LANES), f32),
        vmem((rows // 8, 8, columns), f32),
        vmem((n_enc, cap, columns), bf16),
        vmem((rows // 8, 8, columns), f32),
        vmem((rows // 8, 8, LANES), f32),
        vmem((RING, per_rank, rows, UNIT), bf16),
        vmem((RING, per_rank, rows, UNIT), bf16),
        vmem((RING, per_rank, rows, UNIT), f32),
        vmem((2, per_rank, rows // 2, UNIT), bf16),
        vmem((2, per_rank, rows // 2, UNIT), bf16),
        vmem((2, 2, per_rank, rows // 2, UNIT), bf16),
        vmem((2, 2, per_rank, rows // 2, UNIT), bf16),
        vmem((n_enc, cap, own), bf16),
        vmem((n_llm, n_tp, q_rows, LANES), f32),
        vmem((n_llm, n_tp, q_rows, LANES), f32),
        vmem((q_rows, LANES), f32),
        vmem((n_enc, q_rows, LANES), f32),
        vmem((q_rows, LANES), f32),
        vmem((2, reach, cap, columns), bf16),
        *[dma((n_enc,))] * 6,
        *[dma((n_llm, n_tp))] * 2,
        *[dma((n_llm,))] * 2,
        *[dma((2, reach))] * 2,
        *[dma((RING,))] * 2,
        *[dma((2,))] * 2,
        *[dma((2, 2))] * 2,
        *[dma((2, reach))] * 2,
        dma((9,)),
    ]
    results = (
        jax.ShapeDtypeStruct((1, 1, n_enc, cap, columns), bf16),
        jax.ShapeDtypeStruct((1, 1, n_enc, cap, own), bf16),
        jax.ShapeDtypeStruct((n_llm, q_rows, LANES), f32),
    )
    parts = pl.pallas_call(
        kernel,
        out_shape=results,
        in_specs=[in_hbm] * 6,
        out_specs=[any_space] * 3,
        scratch_shapes=scratch,
        compiler_params=pltpu.CompilerParams(
            collective_id=0, has_side_effects=True, vmem_limit_bytes=48 << 20
        ),
    )(
        *[
            pltpu.with_memory_space_constraint(value, pltpu.HBM)
            for value in (
                counts,
                merger_bias.reshape(1, features),
                norm_gain.reshape(units, 1, UNIT),
                visual,
                kv_weight.reshape(units, UNIT, columns),
                kv_cotangent,
            )
        ]
    )
    key_values, visual_grad, bias_grad = pl.pallas_call(
        write_back,
        out_shape=results,
        in_specs=[any_space] * 3,
        out_specs=[any_space] * 3,
        scratch_shapes=[dma((3,))],
    )(*[pltpu.with_memory_space_constraint(part, pltpu.VMEM) for part in parts])
    return (key_values, visual_grad, bias_grad.reshape(own))


def solution(mesh):
    return jax.shard_map(
        per_device,
        mesh=mesh,
        in_specs=(
            P("enc", "llm", None, None, None),
            P("enc", "llm", None),
            P(),
            P(),
            P(None, "tp"),
            P("enc", "llm", None, None, "tp"),
        ),
        out_specs=(P("enc", "llm", None, None, "tp"), P("enc", "llm", None, None, "tp"), P("tp")),
        check_vma=False,
    )
```

```python
import functools

import jax
import jax.numpy as jnp
from jax import lax
from jax.experimental import pallas as pl
from jax.experimental.pallas import tpu as pltpu
from jax.sharding import PartitionSpec as P

RING = 4
LANES = 128
UNIT = 256


def remote(src, dst, send, recv, **where):
    return pltpu.make_async_remote_copy(
        src_ref=src,
        dst_ref=dst,
        send_sem=send,
        recv_sem=recv,
        device_id=where,
        device_id_type=pl.DeviceIdType.MESH,
    )


def kernel(
    counts_hbm, bias_hbm, gain_hbm, vis_hbm, w_hbm, cot_hbm,
    kv_out, vg_out, bg_out,
    counts, bias, gain, vis, w, cot_own, cot_in, hop, xs, xn, inv, proj, kv_own, masked, coef,
    s1, r1, acc, s2, r2, s3, r3, vg,
    p_own, p_in, z_own, z_in, f_own, kv_hop,
    cot_s, cot_r, kv_s, kv_r, z_s, z_r, p_s, p_r, f_s, f_r, kv_hop_s, kv_hop_r,
    s1_s, s1_r, s2_s, s2_r, s3_s, s3_r, hop_s, hop_r, loc,
):
    n_enc, n_llm = lax.axis_size("enc"), lax.axis_size("llm")
    n_tp = lax.axis_size("tp")
    me, group, rank = lax.axis_index("enc"), lax.axis_index("llm"), lax.axis_index("tp")
    chip, core = rank // 2, rank % 2
    units = w.shape[0]
    per_rank = units // n_tp
    features = units * UNIT
    rows = n_enc * 4
    pairs = n_enc // 2

    reach = n_enc // 4

    def at_step(d):
        return lax.rem(me + d + n_enc, n_enc)

    barrier = pltpu.get_barrier_semaphore()

    @pl.loop(0, reach)
    def _(i):
        d = reach - i
        pl.semaphore_signal(barrier, 1, device_id={"enc": at_step(d)})
        pl.semaphore_signal(barrier, 1, device_id={"enc": at_step(-d)})

    plane = n_llm * n_tp
    q_rows = 8 // n_llm

    def in_plane(i):
        place = lax.rem(group * n_tp + rank + 1 + i, plane)
        return place // n_tp, lax.rem(place, n_tp)

    @pl.loop(0, plane - 1)
    def _(i):
        g, t = in_plane(i)
        pl.semaphore_signal(barrier, 1, device_id={"llm": g, "tp": t})

    loads = [
        pltpu.make_async_copy(src, dst, loc.at[i])
        for i, (src, dst) in enumerate(
            (
                (vis_hbm.at[0, 0], vis),
                (bias_hbm, bias),
                (gain_hbm, gain),
                (cot_hbm.at[0, 0], cot_own),
                (counts_hbm, counts),
                (w_hbm, w),
            )
        )
    ]
    for load in loads:
        load.start()

    for load in loads[:3]:
        load.wait()

    @pl.loop(0, pairs // 2)
    def _(g):
        for h in range(2):
            i = g * 2 + h
            squares = jnp.zeros((8, UNIT), jnp.float32)
            for u in range(units):
                cols = slice(u * UNIT, (u + 1) * UNIT)
                add = bias[:, cols]
                xs[u, i, 0:4, :] = vis[2 * i, :, cols].astype(jnp.float32) + add
                xs[u, i, 4:8, :] = vis[2 * i + 1, :, cols].astype(jnp.float32) + add
                x = xs[u, i]
                squares = squares + x * x
            mean = jnp.sum(squares, axis=1, keepdims=True) * (1.0 / features)
            inv[i] = jnp.broadcast_to(lax.rsqrt(mean + 1e-06), (8, LANES))
        scale = inv[pl.ds(2 * g, 2)].reshape(16, LANES)[:, :1]
        for u in range(units):
            x = xs[u, pl.ds(2 * g, 2)].reshape(16, UNIT)
            xn[u, g] = (x * scale * gain[u]).astype(jnp.bfloat16)

    for load in loads[3:5]:
        load.wait()
    pl.semaphore_wait(barrier, 2 * reach + plane - 1)

    def cot_copy(to, at):
        return remote(cot_own.at[to], cot_in.at[at], cot_s.at[to], cot_r.at[at], enc=to)

    def away(side, d):
        return at_step(d - 2 * side * d)

    def out_copy(side, q):
        to = away(side, reach + q)
        return remote(
            cot_own.at[to], hop.at[side, q - 1], cot_s.at[to], hop_r.at[side, q - 1],
            enc=away(side, reach),
        )

    def on_copy(side, q):
        origin = away(side, -reach)
        return remote(
            hop.at[side, q - 1], cot_in.at[origin], hop_s.at[side, q - 1], cot_r.at[origin],
            enc=away(side, q),
        )

    @pl.loop(0, reach)
    def _(i):
        out_copy(0, reach - i).start()

        @pl.when(i > 0)
        def _():
            out_copy(1, reach - i).start()

    @pl.loop(0, reach)
    def _(i):
        for side in range(2):
            cot_copy(away(side, reach - i), me).start()

    cot_in[me] = cot_own[me]

    loads[5].wait()
    proj[...] = jnp.zeros_like(proj)
    step_units = 4

    @pl.loop(0, units // step_units)
    def _(t):
        total = jnp.zeros((rows, UNIT), jnp.float32)
        for k in range(step_units):
            u = t * step_units + k
            total = total + jnp.dot(
                xn[u].reshape(rows, UNIT), w[u], preferred_element_type=jnp.float32
            )
        proj[...] += total.reshape(proj.shape)

    slot = lax.broadcasted_iota(jnp.int32, (4, UNIT), 0)

    @pl.loop(0, pairs)
    def _(i):
        for h in range(2):
            rows4 = proj[i, 4 * h : 4 * h + 4, :]
            kept = jnp.where(slot < counts[0, 0, 2 * i + h], rows4, 0.0)
            kv_own[2 * i + h] = kept.astype(jnp.bfloat16)

    @pl.loop(0, reach)
    def _(i):
        out_copy(0, reach - i).wait_recv()
        on_copy(0, reach - i).start()

        @pl.when(i > 0)
        def _():
            out_copy(1, reach - i).wait_recv()
            on_copy(1, reach - i).start()

    def kv_copy(to, at):
        return remote(kv_own.at[to], kv_out.at[0, 0, at], kv_s.at[to], kv_r.at[at], enc=to)

    def kv_out_copy(side, q):
        to = away(side, reach + q)
        return remote(
            kv_own.at[to], kv_hop.at[side, q - 1], kv_s.at[to], kv_hop_r.at[side, q - 1],
            enc=away(side, reach),
        )

    def kv_on_copy(side, q):
        origin = away(side, -reach)
        return remote(
            kv_hop.at[side, q - 1], kv_out.at[0, 0, origin], kv_hop_s.at[side, q - 1],
            kv_r.at[origin], enc=away(side, q),
        )

    @pl.loop(0, reach)
    def _(i):
        kv_out_copy(0, reach - i).start()

        @pl.when(i > 0)
        def _():
            kv_out_copy(1, reach - i).start()

    @pl.loop(0, reach)
    def _(i):
        for side in range(2):
            kv_copy(away(side, reach - i), me).start()

    kv_self = pltpu.make_async_copy(kv_own.at[me], kv_out.at[0, 0, me], loc.at[6])
    kv_self.start()

    @pl.loop(0, pairs)
    def _(n):
        step = (n + 1) // 2
        i = lax.rem(me // 2 + step * (1 - 2 * lax.rem(n, 2)) + pairs, pairs)
        for h in range(2):
            other = 2 * i + h

            @pl.when(other != me)
            def _():
                cot_copy(other, other).wait_recv()

        for h in range(2):
            got = cot_in[2 * i + h].astype(jnp.float32)
            masked[i, 4 * h : 4 * h + 4, :] = jnp.where(slot < counts[0, 0, 2 * i + h], got, 0.0)
        dots = jnp.sum(masked[i] * proj[i], axis=1, keepdims=True)
        coef[i] = inv[i] * inv[i] * jnp.broadcast_to(dots, (8, LANES)) * (1.0 / features)

    def term(u):
        cot16 = masked[...].reshape(rows, UNIT).astype(jnp.bfloat16)
        grad = lax.dot_general(
            cot16, w[u], (((1,), (1,)), ((), ())), preferred_element_type=jnp.float32
        )
        a = inv[...].reshape(rows, LANES)[:, :1]
        b = coef[...].reshape(rows, LANES)[:, :1]
        return a * gain[u] * grad - xs[u].reshape(rows, UNIT) * b

    def column_sums(j, v, part):
        total = jnp.sum(part, axis=0, keepdims=True)
        for k in range(UNIT // LANES):
            g, r = divmod(v * (UNIT // LANES) + k, q_rows)
            p_own[g, j, r : r + 1, :] = total[:, k * LANES : (k + 1) * LANES]

    def s1_copy(k):
        return remote(s1.at[k], r1.at[k], s1_s.at[k], s1_r.at[k], tp=rank + 1 - 2 * core)

    order = (2, 1, 3, 0)
    for k in order:
        j = lax.rem(chip + k, RING) * 2 + 1 - core
        for v in range(per_rank):
            part = term(j * per_rank + v)
            s1[k, v] = part.astype(jnp.bfloat16)
            column_sums(j, v, part)
    for k in order:
        j = lax.rem(chip + k, RING) * 2 + core
        for v in range(per_rank):
            part = term(j * per_rank + v)
            acc[k, v] = part
            column_sums(j, v, part)

    def p_copy(g, t, at_g, at_t):
        return remote(
            p_own.at[g, t], p_in.at[at_g, at_t], p_s.at[g, t], p_r.at[at_g, at_t], llm=g, tp=t
        )

    @pl.loop(0, plane - 1)
    def _(i):
        p_copy(*in_plane(i), group, rank).start()

    p_in[group, rank] = p_own[group, rank]
    for k in order:
        s1_copy(k).start()

    @pl.loop(0, plane - 1)
    def _(i):
        g, t = in_plane(i)
        p_copy(g, t, g, t).wait_recv()

    q = jnp.zeros((q_rows, LANES), jnp.float32)
    for g in range(n_llm):
        for t in range(n_tp):
            q = q + p_in[g, t]
    z_own[...] = q

    def z_copy(other, at):
        return remote(z_own, z_in.at[at], z_s.at[other], z_r.at[at], enc=other)

    @pl.loop(0, n_enc - 1)
    def _(i):
        step = (i + 1) // 2
        z_copy(lax.rem(me + n_enc // 2 + step * (1 - 2 * lax.rem(i, 2)), n_enc), me).start()

    z_in[me] = q

    @pl.loop(0, reach)
    def _(i):
        kv_out_copy(0, reach - i).wait_recv()
        kv_on_copy(0, reach - i).start()

        @pl.when(i > 0)
        def _():
            kv_out_copy(1, reach - i).wait_recv()
            kv_on_copy(1, reach - i).start()

    half = rows // 2

    def pair(k):
        s1_copy(k).wait_recv()
        for v in range(per_rank):
            acc[k, v] += r1[k, v].astype(jnp.float32)

    up = lax.rem(chip + 1, RING) * 2 + core
    down = lax.rem(chip + RING - 1, RING) * 2 + core

    def s2_copy(h):
        return remote(s2.at[h], r2.at[h], s2_s.at[h], s2_r.at[h], tp=(up, down)[h])

    def s3_copy(side, h):
        return remote(
            s3.at[side, h], r3.at[side, h], s3_s.at[side, h], s3_r.at[side, h], tp=(up, down)[side]
        )

    def fill(dst, k, h):
        for v in range(per_rank):
            dst[v] = acc[k, v, h * half : (h + 1) * half, :].astype(jnp.bfloat16)

    pair(2)
    for h in range(2):
        fill(s2.at[h], 2, h)
        s2_copy(h).start()
    for side, k in ((0, 1), (1, 3)):
        pair(k)
        fill(s3.at[side, 1 - side], k, 1 - side)
        s3_copy(side, 1 - side).start()

    pair(0)

    for side, k in ((0, 1), (1, 3)):
        s2_copy(side).wait_recv()
        for v in range(per_rank):
            acc[k, v, side * half : (side + 1) * half, :] += r2[side, v].astype(jnp.float32)
        fill(s3.at[side, side], k, side)
        s3_copy(side, side).start()

    for h in range(2):
        for side in range(2):
            s3_copy(side, h).wait_recv()
        for v in range(per_rank):
            total = acc[0, v, h * half : (h + 1) * half, :] + (
                r3[0, h, v].astype(jnp.float32) + r3[1, h, v].astype(jnp.float32)
            )
            acc[0, v, h * half : (h + 1) * half, :] = total
    for b in range(n_enc):
        for v in range(per_rank):
            vg[b, :, v * UNIT : (v + 1) * UNIT] = acc[0, v, 4 * b : 4 * b + 4, :].astype(jnp.bfloat16)
    put_vg = pltpu.make_async_copy(vg, vg_out.at[0, 0], loc.at[7])
    put_vg.start()

    @pl.loop(0, n_enc - 1)
    def _(i):
        other = lax.rem(me + 1 + i, n_enc)
        z_copy(other, other).wait_recv()

    q = z_in[0]
    for s in range(1, n_enc):
        q = q + z_in[s]
    f_own[...] = q

    def f_copy(other, at):
        return remote(f_own, bg_out.at[at], f_s.at[other], f_r.at[at], llm=other)

    for d in range(1, n_llm):
        f_copy(lax.rem(group + d, n_llm), group).start()
    put_f = pltpu.make_async_copy(f_own, bg_out.at[group], loc.at[8])
    put_f.start()

    put_vg.wait()
    kv_self.wait()
    put_f.wait()

    @pl.loop(0, n_enc - 1)
    def _(i):
        other = lax.rem(me + 1 + i, n_enc)
        kv_copy(other, other).wait_recv()
        kv_copy(other, me).wait_send()
        cot_copy(other, me).wait_send()
        z_copy(other, me).wait_send()

    @pl.loop(0, reach)
    def _(i):
        on_copy(0, reach - i).wait_send()
        kv_on_copy(0, reach - i).wait_send()

        @pl.when(i > 0)
        def _():
            on_copy(1, reach - i).wait_send()
            kv_on_copy(1, reach - i).wait_send()

    @pl.loop(0, plane - 1)
    def _(i):
        p_copy(*in_plane(i), group, rank).wait_send()

    for k in range(RING):
        s1_copy(k).wait_send()
    for side in range(2):
        s2_copy(side).wait_send()
        for h in range(2):
            s3_copy(side, h).wait_send()
    for d in range(1, n_llm):
        other = lax.rem(group + d, n_llm)
        f_copy(other, group).wait_send()
        f_copy(other, other).wait_recv()


def write_back(kv, vg, bg, kv_out, vg_out, bg_out, sems):
    puts = [
        pltpu.make_async_copy(src, dst, sems.at[i])
        for i, (src, dst) in enumerate(((vg, vg_out), (kv, kv_out), (bg, bg_out)))
    ]
    for put in puts:
        put.start()
    for put in puts:
        put.wait()


def per_device(visual, counts, merger_bias, norm_gain, kv_weight, kv_cotangent):
    n_enc, cap, features = visual.shape[2:]
    columns = kv_weight.shape[1]
    n_llm, n_tp = lax.axis_size("llm"), lax.axis_size("tp")
    units = features // UNIT
    per_rank = units // n_tp
    rows = n_enc * cap
    own = features // n_tp
    q_rows = 8 // n_llm
    f32, bf16 = jnp.float32, jnp.bfloat16
    vmem, dma = pltpu.VMEM, pltpu.SemaphoreType.DMA
    any_space = pl.BlockSpec(memory_space=pl.ANY)
    in_hbm = any_space
    reach = n_enc // 4
    scratch = [
        pltpu.SMEM((1, 1, n_enc), jnp.int32),
        vmem((1, features), f32),
        vmem((units, 1, UNIT), f32),
        vmem((n_enc, cap, features), bf16),
        vmem((units, UNIT, columns), bf16),
        vmem((n_enc, cap, columns), bf16),
        vmem((n_enc, cap, columns), bf16),
        vmem((2, reach, cap, columns), bf16),
        vmem((units, rows // 8, 8, UNIT), f32),
        vmem((units, rows // 16, 16, UNIT), bf16),
        vmem((rows // 8, 8, LANES), f32),
        vmem((rows // 8, 8, columns), f32),
        vmem((n_enc, cap, columns), bf16),
        vmem((rows // 8, 8, columns), f32),
        vmem((rows // 8, 8, LANES), f32),
        vmem((RING, per_rank, rows, UNIT), bf16),
        vmem((RING, per_rank, rows, UNIT), bf16),
        vmem((RING, per_rank, rows, UNIT), f32),
        vmem((2, per_rank, rows // 2, UNIT), bf16),
        vmem((2, per_rank, rows // 2, UNIT), bf16),
        vmem((2, 2, per_rank, rows // 2, UNIT), bf16),
        vmem((2, 2, per_rank, rows // 2, UNIT), bf16),
        vmem((n_enc, cap, own), bf16),
        vmem((n_llm, n_tp, q_rows, LANES), f32),
        vmem((n_llm, n_tp, q_rows, LANES), f32),
        vmem((q_rows, LANES), f32),
        vmem((n_enc, q_rows, LANES), f32),
        vmem((q_rows, LANES), f32),
        vmem((2, reach, cap, columns), bf16),
        *[dma((n_enc,))] * 6,
        *[dma((n_llm, n_tp))] * 2,
        *[dma((n_llm,))] * 2,
        *[dma((2, reach))] * 2,
        *[dma((RING,))] * 2,
        *[dma((2,))] * 2,
        *[dma((2, 2))] * 2,
        *[dma((2, reach))] * 2,
        dma((9,)),
    ]
    results = (
        jax.ShapeDtypeStruct((1, 1, n_enc, cap, columns), bf16),
        jax.ShapeDtypeStruct((1, 1, n_enc, cap, own), bf16),
        jax.ShapeDtypeStruct((n_llm, q_rows, LANES), f32),
    )
    parts = pl.pallas_call(
        kernel,
        out_shape=results,
        in_specs=[in_hbm] * 6,
        out_specs=[any_space] * 3,
        scratch_shapes=scratch,
        compiler_params=pltpu.CompilerParams(
            collective_id=0, has_side_effects=True, vmem_limit_bytes=48 << 20
        ),
    )(
        *[
            pltpu.with_memory_space_constraint(value, pltpu.HBM)
            for value in (
                counts,
                merger_bias.reshape(1, features),
                norm_gain.reshape(units, 1, UNIT),
                visual,
                kv_weight.reshape(units, UNIT, columns),
                kv_cotangent,
            )
        ]
    )
    key_values, visual_grad, bias_grad = pl.pallas_call(
        write_back,
        out_shape=results,
        in_specs=[any_space] * 3,
        out_specs=[any_space] * 3,
        scratch_shapes=[dma((3,))],
    )(*[pltpu.with_memory_space_constraint(part, pltpu.VMEM) for part in parts])
    return (key_values, visual_grad, bias_grad.reshape(own))


def solution(mesh):
    return jax.shard_map(
        per_device,
        mesh=mesh,
        in_specs=(
            P("enc", "llm", None, None, None),
            P("enc", "llm", None),
            P(),
            P(),
            P(None, "tp"),
            P("enc", "llm", None, None, "tp"),
        ),
        out_specs=(P("enc", "llm", None, None, "tp"), P("enc", "llm", None, None, "tp"), P("tp")),
        check_vma=False,
    )
```

```python
import functools

import jax
import jax.numpy as jnp
from jax import lax
from jax.experimental import pallas as pl
from jax.experimental.pallas import tpu as pltpu
from jax.sharding import PartitionSpec as P

RING = 4
LANES = 128
UNIT = 256


def remote(src, dst, send, recv, **where):
    return pltpu.make_async_remote_copy(
        src_ref=src,
        dst_ref=dst,
        send_sem=send,
        recv_sem=recv,
        device_id=where,
        device_id_type=pl.DeviceIdType.MESH,
    )


def wide(v):
    return jnp.concatenate([v] * (UNIT // LANES), axis=1)


def kernel(
    counts_hbm, bias_hbm, gain_hbm, vis_hbm, w_hbm, cot_hbm,
    kv_out, vg_out, bg_out,
    counts, bias, gain, vis, w, cot_own, cot_in, hop, xs, xn, inv, proj, kv_own, masked, coef,
    s1, r1, acc, s2, r2, s3, r3, vg,
    p_own, p_in, z_own, z_in, f_own, kv_hop,
    cot_s, cot_r, kv_s, kv_r, z_s, z_r, p_s, p_r, f_s, f_r, kv_hop_s, kv_hop_r,
    s1_s, s1_r, s2_s, s2_r, s3_s, s3_r, hop_s, hop_r, loc, deep,
):
    n_enc, n_llm = lax.axis_size("enc"), lax.axis_size("llm")
    n_tp = lax.axis_size("tp")
    me, group, rank = lax.axis_index("enc"), lax.axis_index("llm"), lax.axis_index("tp")
    chip, core = rank // 2, rank % 2
    units = w.shape[0]
    per_rank = units // n_tp
    features = units * UNIT
    rows = n_enc * 4
    pairs = n_enc // 2

    far = hop.shape[1]
    reach = n_enc // 2 - far

    def at_step(d):
        return lax.rem(me + d + n_enc, n_enc)

    barrier = pltpu.get_barrier_semaphore()

    @pl.loop(0, reach)
    def _(i):
        d = reach - i
        pl.semaphore_signal(barrier, 1, device_id={"enc": at_step(d)})
        pl.semaphore_signal(barrier, 1, device_id={"enc": at_step(-d)})

    plane = n_llm * n_tp
    q_rows = 8 // n_llm

    def in_plane(i):
        place = lax.rem(group * n_tp + rank + 1 + i, plane)
        return place // n_tp, lax.rem(place, n_tp)

    @pl.loop(0, plane - 1)
    def _(i):
        g, t = in_plane(i)
        pl.semaphore_signal(barrier, 1, device_id={"llm": g, "tp": t})

    loads = [
        pltpu.make_async_copy(src, dst, loc.at[i])
        for i, (src, dst) in enumerate(
            (
                (vis_hbm.at[0, 0], vis),
                (bias_hbm, bias),
                (gain_hbm, gain),
                (cot_hbm.at[0, 0], cot_own),
                (counts_hbm, counts),
                (w_hbm, w),
            )
        )
    ]
    for load in loads:
        load.start()

    for load in loads[:3]:
        load.wait()

    @pl.loop(0, pairs // 2)
    def _(g):
        for h in range(2):
            i = g * 2 + h
            squares = jnp.zeros((8, UNIT), jnp.float32)
            for u in range(units):
                cols = slice(u * UNIT, (u + 1) * UNIT)
                add = bias[:, cols]
                xs[u, i, 0:4, :] = vis[2 * i, :, cols].astype(jnp.float32) + add
                xs[u, i, 4:8, :] = vis[2 * i + 1, :, cols].astype(jnp.float32) + add
                x = xs[u, i]
                squares = squares + x * x
            mean = jnp.sum(squares, axis=1, keepdims=True) * (1.0 / features)
            inv[i] = jnp.broadcast_to(lax.rsqrt(mean + 1e-06), (8, LANES))
        scale = wide(inv[pl.ds(2 * g, 2)].reshape(16, LANES))
        for u in range(units):
            x = xs[u, pl.ds(2 * g, 2)].reshape(16, UNIT)
            xn[u, g] = (x * scale * gain[u]).astype(jnp.bfloat16)

    for load in loads[3:5]:
        load.wait()
    pl.semaphore_wait(barrier, 2 * reach + plane - 1)
    for side in range(2):
        pl.semaphore_signal(deep, 1, device_id={"enc": at_step(reach - 2 * side * reach)})

    def cot_copy(to, at):
        return remote(cot_own.at[to], cot_in.at[at], cot_s.at[to], cot_r.at[at], enc=to)

    def away(side, d):
        return at_step(d - 2 * side * d)

    def out_copy(side, q):
        to = away(side, reach + q)
        return remote(
            cot_own.at[to], hop.at[side, q - 1], cot_s.at[to], hop_r.at[side, q - 1],
            enc=away(side, reach),
        )

    def on_copy(side, q):
        origin = away(side, -reach)
        return remote(
            hop.at[side, q - 1], cot_in.at[origin], hop_s.at[side, q - 1], cot_r.at[origin],
            enc=away(side, q),
        )

    @pl.loop(0, far)
    def _(i):
        out_copy(0, far - i).start()

        @pl.when(i > 0)
        def _():
            out_copy(1, far - i).start()

    @pl.loop(0, reach)
    def _(i):
        for side in range(2):
            cot_copy(away(side, reach - i), me).start()

    cot_in[me] = cot_own[me]

    loads[5].wait()
    proj[...] = jnp.zeros_like(proj)
    step_units = 4

    @pl.loop(0, units // step_units)
    def _(t):
        total = jnp.zeros((rows, UNIT), jnp.float32)
        for k in range(step_units):
            u = t * step_units + k
            total = total + jnp.dot(
                xn[u].reshape(rows, UNIT), w[u], preferred_element_type=jnp.float32
            )
        proj[...] += total.reshape(proj.shape)

    slot = lax.broadcasted_iota(jnp.int32, (4, UNIT), 0)

    @pl.loop(0, pairs)
    def _(i):
        for h in range(2):
            rows4 = proj[i, 4 * h : 4 * h + 4, :]
            kept = jnp.where(slot < counts[0, 0, 2 * i + h], rows4, 0.0)
            kv_own[2 * i + h] = kept.astype(jnp.bfloat16)

    pl.semaphore_wait(deep, 2)

    @pl.loop(0, far)
    def _(i):
        out_copy(0, far - i).wait_recv()
        on_copy(0, far - i).start()

        @pl.when(i > 0)
        def _():
            out_copy(1, far - i).wait_recv()
            on_copy(1, far - i).start()

    def kv_copy(to, at):
        return remote(kv_own.at[to], kv_out.at[0, 0, at], kv_s.at[to], kv_r.at[at], enc=to)

    def kv_out_copy(side, q):
        to = away(side, reach + q)
        return remote(
            kv_own.at[to], kv_hop.at[side, q - 1], kv_s.at[to], kv_hop_r.at[side, q - 1],
            enc=away(side, reach),
        )

    def kv_on_copy(side, q):
        origin = away(side, -reach)
        return remote(
            kv_hop.at[side, q - 1], kv_out.at[0, 0, origin], kv_hop_s.at[side, q - 1],
            kv_r.at[origin], enc=away(side, q),
        )

    @pl.loop(0, far)
    def _(i):
        kv_out_copy(0, far - i).start()

        @pl.when(i > 0)
        def _():
            kv_out_copy(1, far - i).start()

    @pl.loop(0, reach)
    def _(i):
        for side in range(2):
            kv_copy(away(side, reach - i), me).start()

    kv_self = pltpu.make_async_copy(kv_own.at[me], kv_out.at[0, 0, me], loc.at[6])
    kv_self.start()

    @pl.loop(0, pairs)
    def _(n):
        step = (n + 1) // 2
        i = lax.rem(me // 2 + step * (1 - 2 * lax.rem(n, 2)) + pairs, pairs)
        for h in range(2):
            other = 2 * i + h

            @pl.when(other != me)
            def _():
                cot_copy(other, other).wait_recv()

        for h in range(2):
            got = cot_in[2 * i + h].astype(jnp.float32)
            masked[i, 4 * h : 4 * h + 4, :] = jnp.where(slot < counts[0, 0, 2 * i + h], got, 0.0)
        dots = jnp.sum(masked[i] * proj[i], axis=1, keepdims=True)
        coef[i] = inv[i] * inv[i] * jnp.broadcast_to(dots, (8, LANES)) * (1.0 / features)

    def term(u):
        cot16 = masked[...].reshape(rows, UNIT).astype(jnp.bfloat16)
        grad = lax.dot_general(
            cot16, w[u], (((1,), (1,)), ((), ())), preferred_element_type=jnp.float32
        )
        a, b = wide(inv[...].reshape(rows, LANES)), wide(coef[...].reshape(rows, LANES))
        return a * gain[u] * grad - xs[u].reshape(rows, UNIT) * b

    def column_sums(j, v, part):
        total = jnp.sum(part, axis=0, keepdims=True)
        for k in range(UNIT // LANES):
            g, r = divmod(v * (UNIT // LANES) + k, q_rows)
            p_own[g, j, r : r + 1, :] = total[:, k * LANES : (k + 1) * LANES]

    def s1_copy(k):
        return remote(s1.at[k], r1.at[k], s1_s.at[k], s1_r.at[k], tp=rank + 1 - 2 * core)

    order = (2, 1, 3, 0)
    for k in order:
        j = lax.rem(chip + k, RING) * 2 + 1 - core
        for v in range(per_rank):
            part = term(j * per_rank + v)
            s1[k, v] = part.astype(jnp.bfloat16)
            column_sums(j, v, part)
    for k in order:
        j = lax.rem(chip + k, RING) * 2 + core
        for v in range(per_rank):
            part = term(j * per_rank + v)
            acc[k, v] = part
            column_sums(j, v, part)

    def p_copy(g, t, at_g, at_t):
        return remote(
            p_own.at[g, t], p_in.at[at_g, at_t], p_s.at[g, t], p_r.at[at_g, at_t], llm=g, tp=t
        )

    @pl.loop(0, plane - 1)
    def _(i):
        p_copy(*in_plane(i), group, rank).start()

    p_in[group, rank] = p_own[group, rank]
    for k in order:
        s1_copy(k).start()

    @pl.loop(0, plane - 1)
    def _(i):
        g, t = in_plane(i)
        p_copy(g, t, g, t).wait_recv()

    q = jnp.zeros((q_rows, LANES), jnp.float32)
    for g in range(n_llm):
        for t in range(n_tp):
            q = q + p_in[g, t]
    z_own[...] = q

    def z_copy(other, at):
        return remote(z_own, z_in.at[at], z_s.at[other], z_r.at[at], enc=other)

    @pl.loop(0, n_enc - 1)
    def _(i):
        step = (i + 1) // 2
        z_copy(lax.rem(me + n_enc // 2 + step * (1 - 2 * lax.rem(i, 2)), n_enc), me).start()

    z_in[me] = q

    @pl.loop(0, far)
    def _(i):
        kv_out_copy(0, far - i).wait_recv()
        kv_on_copy(0, far - i).start()

        @pl.when(i > 0)
        def _():
            kv_out_copy(1, far - i).wait_recv()
            kv_on_copy(1, far - i).start()

    half = rows // 2

    def pair(k):
        s1_copy(k).wait_recv()
        for v in range(per_rank):
            acc[k, v] += r1[k, v].astype(jnp.float32)

    up = lax.rem(chip + 1, RING) * 2 + core
    down = lax.rem(chip + RING - 1, RING) * 2 + core

    def s2_copy(h):
        return remote(s2.at[h], r2.at[h], s2_s.at[h], s2_r.at[h], tp=(up, down)[h])

    def s3_copy(side, h):
        return remote(
            s3.at[side, h], r3.at[side, h], s3_s.at[side, h], s3_r.at[side, h], tp=(up, down)[side]
        )

    def fill(dst, k, h):
        for v in range(per_rank):
            dst[v] = acc[k, v, h * half : (h + 1) * half, :].astype(jnp.bfloat16)

    pair(2)
    for h in range(2):
        fill(s2.at[h], 2, h)
        s2_copy(h).start()
    for side, k in ((0, 1), (1, 3)):
        pair(k)
        fill(s3.at[side, 1 - side], k, 1 - side)
        s3_copy(side, 1 - side).start()

    pair(0)

    for side, k in ((0, 1), (1, 3)):
        s2_copy(side).wait_recv()
        for v in range(per_rank):
            acc[k, v, side * half : (side + 1) * half, :] += r2[side, v].astype(jnp.float32)
        fill(s3.at[side, side], k, side)
        s3_copy(side, side).start()

    for h in range(2):
        for side in range(2):
            s3_copy(side, h).wait_recv()
        for v in range(per_rank):
            total = acc[0, v, h * half : (h + 1) * half, :] + (
                r3[0, h, v].astype(jnp.float32) + r3[1, h, v].astype(jnp.float32)
            )
            acc[0, v, h * half : (h + 1) * half, :] = total
    for b in range(n_enc):
        for v in range(per_rank):
            vg[b, :, v * UNIT : (v + 1) * UNIT] = acc[0, v, 4 * b : 4 * b + 4, :].astype(jnp.bfloat16)
    put_vg = pltpu.make_async_copy(vg, vg_out.at[0, 0], loc.at[7])
    put_vg.start()

    @pl.loop(0, n_enc - 1)
    def _(i):
        other = lax.rem(me + 1 + i, n_enc)
        z_copy(other, other).wait_recv()

    q = z_in[0]
    for s in range(1, n_enc):
        q = q + z_in[s]
    f_own[...] = q

    def f_copy(other, at):
        return remote(f_own, bg_out.at[at], f_s.at[other], f_r.at[at], llm=other)

    for d in range(1, n_llm):
        f_copy(lax.rem(group + d, n_llm), group).start()
    put_f = pltpu.make_async_copy(f_own, bg_out.at[group], loc.at[8])
    put_f.start()

    put_vg.wait()
    kv_self.wait()
    put_f.wait()

    @pl.loop(0, n_enc - 1)
    def _(i):
        other = lax.rem(me + 1 + i, n_enc)
        kv_copy(other, other).wait_recv()
        kv_copy(other, me).wait_send()
        cot_copy(other, me).wait_send()
        z_copy(other, me).wait_send()

    @pl.loop(0, far)
    def _(i):
        on_copy(0, far - i).wait_send()
        kv_on_copy(0, far - i).wait_send()

        @pl.when(i > 0)
        def _():
            on_copy(1, far - i).wait_send()
            kv_on_copy(1, far - i).wait_send()

    @pl.loop(0, plane - 1)
    def _(i):
        p_copy(*in_plane(i), group, rank).wait_send()

    for k in range(RING):
        s1_copy(k).wait_send()
    for side in range(2):
        s2_copy(side).wait_send()
        for h in range(2):
            s3_copy(side, h).wait_send()
    for d in range(1, n_llm):
        other = lax.rem(group + d, n_llm)
        f_copy(other, group).wait_send()
        f_copy(other, other).wait_recv()


def write_back(kv, vg, bg, kv_out, vg_out, bg_out, sems):
    puts = [
        pltpu.make_async_copy(src, dst, sems.at[i])
        for i, (src, dst) in enumerate(((vg, vg_out), (kv, kv_out), (bg, bg_out)))
    ]
    for put in puts:
        put.start()
    for put in puts:
        put.wait()


def per_device(visual, counts, merger_bias, norm_gain, kv_weight, kv_cotangent):
    n_enc, cap, features = visual.shape[2:]
    columns = kv_weight.shape[1]
    n_llm, n_tp = lax.axis_size("llm"), lax.axis_size("tp")
    units = features // UNIT
    per_rank = units // n_tp
    rows = n_enc * cap
    own = features // n_tp
    q_rows = 8 // n_llm
    f32, bf16 = jnp.float32, jnp.bfloat16
    vmem, dma = pltpu.VMEM, pltpu.SemaphoreType.DMA
    any_space = pl.BlockSpec(memory_space=pl.ANY)
    in_hbm = any_space
    far = n_enc // 2 - (n_enc // 2 + 2) // 3
    scratch = [
        pltpu.SMEM((1, 1, n_enc), jnp.int32),
        vmem((1, features), f32),
        vmem((units, 1, UNIT), f32),
        vmem((n_enc, cap, features), bf16),
        vmem((units, UNIT, columns), bf16),
        vmem((n_enc, cap, columns), bf16),
        vmem((n_enc, cap, columns), bf16),
        vmem((2, far, cap, columns), bf16),
        vmem((units, rows // 8, 8, UNIT), f32),
        vmem((units, rows // 16, 16, UNIT), bf16),
        vmem((rows // 8, 8, LANES), f32),
        vmem((rows // 8, 8, columns), f32),
        vmem((n_enc, cap, columns), bf16),
        vmem((rows // 8, 8, columns), f32),
        vmem((rows // 8, 8, LANES), f32),
        vmem((RING, per_rank, rows, UNIT), bf16),
        vmem((RING, per_rank, rows, UNIT), bf16),
        vmem((RING, per_rank, rows, UNIT), f32),
        vmem((2, per_rank, rows // 2, UNIT), bf16),
        vmem((2, per_rank, rows // 2, UNIT), bf16),
        vmem((2, 2, per_rank, rows // 2, UNIT), bf16),
        vmem((2, 2, per_rank, rows // 2, UNIT), bf16),
        vmem((n_enc, cap, own), bf16),
        vmem((n_llm, n_tp, q_rows, LANES), f32),
        vmem((n_llm, n_tp, q_rows, LANES), f32),
        vmem((q_rows, LANES), f32),
        vmem((n_enc, q_rows, LANES), f32),
        vmem((q_rows, LANES), f32),
        vmem((2, far, cap, columns), bf16),
        *[dma((n_enc,))] * 6,
        *[dma((n_llm, n_tp))] * 2,
        *[dma((n_llm,))] * 2,
        *[dma((2, far))] * 2,
        *[dma((RING,))] * 2,
        *[dma((2,))] * 2,
        *[dma((2, 2))] * 2,
        *[dma((2, far))] * 2,
        dma((9,)),
        pltpu.SemaphoreType.REGULAR,
    ]
    results = (
        jax.ShapeDtypeStruct((1, 1, n_enc, cap, columns), bf16),
        jax.ShapeDtypeStruct((1, 1, n_enc, cap, own), bf16),
        jax.ShapeDtypeStruct((n_llm, q_rows, LANES), f32),
    )
    parts = pl.pallas_call(
        kernel,
        out_shape=results,
        in_specs=[in_hbm] * 6,
        out_specs=[any_space] * 3,
        scratch_shapes=scratch,
        compiler_params=pltpu.CompilerParams(
            collective_id=0, has_side_effects=True, vmem_limit_bytes=48 << 20
        ),
    )(
        *[
            pltpu.with_memory_space_constraint(value, pltpu.HBM)
            for value in (
                counts,
                merger_bias.reshape(1, features),
                norm_gain.reshape(units, 1, UNIT),
                visual,
                kv_weight.reshape(units, UNIT, columns),
                kv_cotangent,
            )
        ]
    )
    key_values, visual_grad, bias_grad = pl.pallas_call(
        write_back,
        out_shape=results,
        in_specs=[any_space] * 3,
        out_specs=[any_space] * 3,
        scratch_shapes=[dma((3,))],
    )(*[pltpu.with_memory_space_constraint(part, pltpu.VMEM) for part in parts])
    return (key_values, visual_grad, bias_grad.reshape(own))


def solution(mesh):
    return jax.shard_map(
        per_device,
        mesh=mesh,
        in_specs=(
            P("enc", "llm", None, None, None),
            P("enc", "llm", None),
            P(),
            P(),
            P(None, "tp"),
            P("enc", "llm", None, None, "tp"),
        ),
        out_specs=(P("enc", "llm", None, None, "tp"), P("enc", "llm", None, None, "tp"), P("tp")),
        check_vma=False,
    )
```

```python
import functools

import jax
import jax.numpy as jnp
from jax import lax
from jax.experimental import pallas as pl
from jax.experimental.pallas import tpu as pltpu
from jax.sharding import PartitionSpec as P

RING = 4
LANES = 128
UNIT = 256


def remote(src, dst, send, recv, **where):
    return pltpu.make_async_remote_copy(
        src_ref=src,
        dst_ref=dst,
        send_sem=send,
        recv_sem=recv,
        device_id=where,
        device_id_type=pl.DeviceIdType.MESH,
    )


def wide(v):
    return jnp.concatenate([v] * (UNIT // LANES), axis=1)


def kernel(
    counts_hbm, bias_hbm, gain_hbm, vis_hbm, w_hbm, cot_hbm,
    kv_out, vg_out, bg_out,
    counts, bias, gain, vis, w, cot_own, cot_in, hop, xs, xn, inv, proj, kv_own, masked, coef,
    s1, r1, acc, s2, r2, s3, r3, vg,
    p_own, p_in, z_own, zb_own, z_in, f_own, kv_hop,
    cot_s, cot_r, kv_s, kv_r, z_s, z_r, p_s, p_r, f_s, f_r, kv_hop_s, kv_hop_r,
    s1_s, s1_r, s2_s, s2_r, s3_s, s3_r, hop_s, hop_r, loc, deep,
):
    n_enc, n_llm = lax.axis_size("enc"), lax.axis_size("llm")
    n_tp = lax.axis_size("tp")
    me, group, rank = lax.axis_index("enc"), lax.axis_index("llm"), lax.axis_index("tp")
    chip, core = rank // 2, rank % 2
    units = w.shape[0]
    per_rank = units // n_tp
    features = units * UNIT
    rows = n_enc * 4
    pairs = n_enc // 2

    far = hop.shape[1]
    reach = n_enc // 2 - far

    def at_step(d):
        return lax.rem(me + d + n_enc, n_enc)

    barrier = pltpu.get_barrier_semaphore()

    @pl.loop(0, reach)
    def _(i):
        d = reach - i
        pl.semaphore_signal(barrier, 1, device_id={"enc": at_step(d)})
        pl.semaphore_signal(barrier, 1, device_id={"enc": at_step(-d)})

    plane = n_llm * n_tp
    q_rows = 8 // n_llm

    def in_plane(i):
        place = lax.rem(group * n_tp + rank + 1 + i, plane)
        return place // n_tp, lax.rem(place, n_tp)

    @pl.loop(0, plane - 1)
    def _(i):
        g, t = in_plane(i)
        pl.semaphore_signal(barrier, 1, device_id={"llm": g, "tp": t})

    loads = [
        pltpu.make_async_copy(src, dst, loc.at[i])
        for i, (src, dst) in enumerate(
            (
                (vis_hbm.at[0, 0], vis),
                (bias_hbm, bias),
                (gain_hbm, gain),
                (cot_hbm.at[0, 0], cot_own),
                (counts_hbm, counts),
                (w_hbm, w),
            )
        )
    ]
    for load in loads:
        load.start()

    for load in loads[:3]:
        load.wait()

    @pl.loop(0, pairs // 2)
    def _(g):
        for h in range(2):
            i = g * 2 + h
            squares = jnp.zeros((8, UNIT), jnp.float32)
            for u in range(units):
                cols = slice(u * UNIT, (u + 1) * UNIT)
                add = bias[:, cols]
                xs[u, i, 0:4, :] = vis[2 * i, :, cols].astype(jnp.float32) + add
                xs[u, i, 4:8, :] = vis[2 * i + 1, :, cols].astype(jnp.float32) + add
                x = xs[u, i]
                squares = squares + x * x
            mean = jnp.sum(squares, axis=1, keepdims=True) * (1.0 / features)
            inv[i] = jnp.broadcast_to(lax.rsqrt(mean + 1e-06), (8, LANES))
        scale = wide(inv[pl.ds(2 * g, 2)].reshape(16, LANES))
        for u in range(units):
            x = xs[u, pl.ds(2 * g, 2)].reshape(16, UNIT)
            xn[u, g] = (x * scale * gain[u]).astype(jnp.bfloat16)

    for load in loads[3:5]:
        load.wait()
    pl.semaphore_wait(barrier, 2 * reach + plane - 1)
    for side in range(2):
        pl.semaphore_signal(deep, 1, device_id={"enc": at_step(reach - 2 * side * reach)})

    def cot_copy(to, at):
        return remote(cot_own.at[to], cot_in.at[at], cot_s.at[to], cot_r.at[at], enc=to)

    def away(side, d):
        return at_step(d - 2 * side * d)

    def out_copy(side, q):
        to = away(side, reach + q)
        return remote(
            cot_own.at[to], hop.at[side, q - 1], cot_s.at[to], hop_r.at[side, q - 1],
            enc=away(side, reach),
        )

    def on_copy(side, q):
        origin = away(side, -reach)
        return remote(
            hop.at[side, q - 1], cot_in.at[origin], hop_s.at[side, q - 1], cot_r.at[origin],
            enc=away(side, q),
        )

    @pl.loop(0, far)
    def _(i):
        out_copy(0, far - i).start()

        @pl.when(i > 0)
        def _():
            out_copy(1, far - i).start()

    @pl.loop(0, reach)
    def _(i):
        for side in range(2):
            cot_copy(away(side, reach - i), me).start()

    cot_in[me] = cot_own[me]

    loads[5].wait()
    proj[...] = jnp.zeros_like(proj)
    step_units = 4

    @pl.loop(0, units // step_units)
    def _(t):
        total = jnp.zeros((rows, UNIT), jnp.float32)
        for k in range(step_units):
            u = t * step_units + k
            total = total + jnp.dot(
                xn[u].reshape(rows, UNIT), w[u], preferred_element_type=jnp.float32
            )
        proj[...] += total.reshape(proj.shape)

    slot = lax.broadcasted_iota(jnp.int32, (4, UNIT), 0)

    @pl.loop(0, pairs)
    def _(i):
        for h in range(2):
            rows4 = proj[i, 4 * h : 4 * h + 4, :]
            kept = jnp.where(slot < counts[0, 0, 2 * i + h], rows4, 0.0)
            kv_own[2 * i + h] = kept.astype(jnp.bfloat16)

    pl.semaphore_wait(deep, 2)

    @pl.loop(0, far)
    def _(i):
        out_copy(0, far - i).wait_recv()
        on_copy(0, far - i).start()

        @pl.when(i > 0)
        def _():
            out_copy(1, far - i).wait_recv()
            on_copy(1, far - i).start()

    def kv_copy(to, at):
        return remote(kv_own.at[to], kv_out.at[0, 0, at], kv_s.at[to], kv_r.at[at], enc=to)

    def kv_out_copy(side, q):
        to = away(side, reach + q)
        return remote(
            kv_own.at[to], kv_hop.at[side, q - 1], kv_s.at[to], kv_hop_r.at[side, q - 1],
            enc=away(side, reach),
        )

    def kv_on_copy(side, q):
        origin = away(side, -reach)
        return remote(
            kv_hop.at[side, q - 1], kv_out.at[0, 0, origin], kv_hop_s.at[side, q - 1],
            kv_r.at[origin], enc=away(side, q),
        )

    @pl.loop(0, far)
    def _(i):
        kv_out_copy(0, far - i).start()

        @pl.when(i > 0)
        def _():
            kv_out_copy(1, far - i).start()

    @pl.loop(0, reach)
    def _(i):
        for side in range(2):
            kv_copy(away(side, reach - i), me).start()

    kv_self = pltpu.make_async_copy(kv_own.at[me], kv_out.at[0, 0, me], loc.at[6])
    kv_self.start()

    @pl.loop(0, pairs)
    def _(n):
        step = (n + 1) // 2
        i = lax.rem(me // 2 + step * (1 - 2 * lax.rem(n, 2)) + pairs, pairs)
        for h in range(2):
            other = 2 * i + h

            @pl.when(other != me)
            def _():
                cot_copy(other, other).wait_recv()

        for h in range(2):
            got = cot_in[2 * i + h].astype(jnp.float32)
            masked[i, 4 * h : 4 * h + 4, :] = jnp.where(slot < counts[0, 0, 2 * i + h], got, 0.0)
        dots = jnp.sum(masked[i] * proj[i], axis=1, keepdims=True)
        coef[i] = inv[i] * inv[i] * jnp.broadcast_to(dots, (8, LANES)) * (1.0 / features)

    def term(u):
        cot16 = masked[...].reshape(rows, UNIT).astype(jnp.bfloat16)
        grad = lax.dot_general(
            cot16, w[u], (((1,), (1,)), ((), ())), preferred_element_type=jnp.float32
        )
        a, b = wide(inv[...].reshape(rows, LANES)), wide(coef[...].reshape(rows, LANES))
        return a * gain[u] * grad - xs[u].reshape(rows, UNIT) * b

    def column_sums(j, v, part):
        total = jnp.sum(part, axis=0, keepdims=True)
        for k in range(UNIT // LANES):
            g, r = divmod(v * (UNIT // LANES) + k, q_rows)
            p_own[g, j, r : r + 1, :] = total[:, k * LANES : (k + 1) * LANES]

    def s1_copy(k):
        return remote(s1.at[k], r1.at[k], s1_s.at[k], s1_r.at[k], tp=rank + 1 - 2 * core)

    order = (2, 1, 3, 0)
    for k in order:
        j = lax.rem(chip + k, RING) * 2 + 1 - core
        for v in range(per_rank):
            part = term(j * per_rank + v)
            s1[k, v] = part.astype(jnp.bfloat16)
            column_sums(j, v, part)
    for k in order:
        j = lax.rem(chip + k, RING) * 2 + core
        for v in range(per_rank):
            part = term(j * per_rank + v)
            acc[k, v] = part
            column_sums(j, v, part)

    def p_copy(g, t, at_g, at_t):
        return remote(
            p_own.at[g, t], p_in.at[at_g, at_t], p_s.at[g, t], p_r.at[at_g, at_t], llm=g, tp=t
        )

    @pl.loop(0, plane - 1)
    def _(i):
        p_copy(*in_plane(i), group, rank).start()

    p_in[group, rank] = p_own[group, rank]
    for k in order:
        s1_copy(k).start()

    @pl.loop(0, plane - 1)
    def _(i):
        g, t = in_plane(i)
        p_copy(g, t, g, t).wait_recv()

    q = jnp.zeros((q_rows, LANES), jnp.float32)
    for g in range(n_llm):
        for t in range(n_tp):
            q = q + p_in[g, t]
    z_own[...] = q

    blocks = n_enc // 4
    base, place = me // 4 * 4, lax.rem(me, 4)

    def z_copy(src, other, at):
        return remote(src, z_in.at[at], z_s.at[other], z_r.at[at], enc=other)

    near_block = [base + lax.rem(place + d, 4) for d in (2, 1, 3)]
    steps = sorted(range(1, blocks), key=lambda d: -min(d, blocks - d))
    across = [lax.rem(me + 4 * d, n_enc) for d in steps]
    for other in near_block:
        z_copy(z_own, other, me).start()
    z_in[me] = q
    for other in near_block:
        z_copy(z_own, other, other).wait_recv()
    q = z_in[base]
    for d in range(1, 4):
        q = q + z_in[base + d]
    zb_own[...] = q
    for other in across:
        z_copy(zb_own, other, me).start()
    z_in[me] = q

    @pl.loop(0, far)
    def _(i):
        kv_out_copy(0, far - i).wait_recv()
        kv_on_copy(0, far - i).start()

        @pl.when(i > 0)
        def _():
            kv_out_copy(1, far - i).wait_recv()
            kv_on_copy(1, far - i).start()

    half = rows // 2

    def pair(k):
        s1_copy(k).wait_recv()
        for v in range(per_rank):
            acc[k, v] += r1[k, v].astype(jnp.float32)

    up = lax.rem(chip + 1, RING) * 2 + core
    down = lax.rem(chip + RING - 1, RING) * 2 + core

    def s2_copy(h):
        return remote(s2.at[h], r2.at[h], s2_s.at[h], s2_r.at[h], tp=(up, down)[h])

    def s3_copy(side, h):
        return remote(
            s3.at[side, h], r3.at[side, h], s3_s.at[side, h], s3_r.at[side, h], tp=(up, down)[side]
        )

    def fill(dst, k, h):
        for v in range(per_rank):
            dst[v] = acc[k, v, h * half : (h + 1) * half, :].astype(jnp.bfloat16)

    pair(2)
    for h in range(2):
        fill(s2.at[h], 2, h)
        s2_copy(h).start()
    for side, k in ((0, 1), (1, 3)):
        pair(k)
        fill(s3.at[side, 1 - side], k, 1 - side)
        s3_copy(side, 1 - side).start()

    pair(0)

    for side, k in ((0, 1), (1, 3)):
        s2_copy(side).wait_recv()
        for v in range(per_rank):
            acc[k, v, side * half : (side + 1) * half, :] += r2[side, v].astype(jnp.float32)
        fill(s3.at[side, side], k, side)
        s3_copy(side, side).start()

    for h in range(2):
        for side in range(2):
            s3_copy(side, h).wait_recv()
        for v in range(per_rank):
            total = acc[0, v, h * half : (h + 1) * half, :] + (
                r3[0, h, v].astype(jnp.float32) + r3[1, h, v].astype(jnp.float32)
            )
            acc[0, v, h * half : (h + 1) * half, :] = total
    for b in range(n_enc):
        for v in range(per_rank):
            vg[b, :, v * UNIT : (v + 1) * UNIT] = acc[0, v, 4 * b : 4 * b + 4, :].astype(jnp.bfloat16)
    put_vg = pltpu.make_async_copy(vg, vg_out.at[0, 0], loc.at[7])
    put_vg.start()

    for other in across:
        z_copy(zb_own, other, other).wait_recv()
    q = z_in[place]
    for d in range(1, blocks):
        q = q + z_in[4 * d + place]
    f_own[...] = q

    def f_copy(other, at):
        return remote(f_own, bg_out.at[at], f_s.at[other], f_r.at[at], llm=other)

    for d in range(1, n_llm):
        f_copy(lax.rem(group + d, n_llm), group).start()
    put_f = pltpu.make_async_copy(f_own, bg_out.at[group], loc.at[8])
    put_f.start()

    put_vg.wait()
    kv_self.wait()
    put_f.wait()

    @pl.loop(0, n_enc - 1)
    def _(i):
        other = lax.rem(me + 1 + i, n_enc)
        kv_copy(other, other).wait_recv()
        kv_copy(other, me).wait_send()
        cot_copy(other, me).wait_send()

    @pl.loop(0, far)
    def _(i):
        on_copy(0, far - i).wait_send()
        kv_on_copy(0, far - i).wait_send()

        @pl.when(i > 0)
        def _():
            on_copy(1, far - i).wait_send()
            kv_on_copy(1, far - i).wait_send()

    @pl.loop(0, plane - 1)
    def _(i):
        p_copy(*in_plane(i), group, rank).wait_send()

    for other in near_block:
        z_copy(z_own, other, me).wait_send()
    for other in across:
        z_copy(zb_own, other, me).wait_send()
    for k in range(RING):
        s1_copy(k).wait_send()
    for side in range(2):
        s2_copy(side).wait_send()
        for h in range(2):
            s3_copy(side, h).wait_send()
    for d in range(1, n_llm):
        other = lax.rem(group + d, n_llm)
        f_copy(other, group).wait_send()
        f_copy(other, other).wait_recv()


def write_back(kv, vg, bg, kv_out, vg_out, bg_out, sems):
    puts = [
        pltpu.make_async_copy(src, dst, sems.at[i])
        for i, (src, dst) in enumerate(((vg, vg_out), (kv, kv_out), (bg, bg_out)))
    ]
    for put in puts:
        put.start()
    for put in puts:
        put.wait()


def per_device(visual, counts, merger_bias, norm_gain, kv_weight, kv_cotangent):
    n_enc, cap, features = visual.shape[2:]
    columns = kv_weight.shape[1]
    n_llm, n_tp = lax.axis_size("llm"), lax.axis_size("tp")
    units = features // UNIT
    per_rank = units // n_tp
    rows = n_enc * cap
    own = features // n_tp
    q_rows = 8 // n_llm
    f32, bf16 = jnp.float32, jnp.bfloat16
    vmem, dma = pltpu.VMEM, pltpu.SemaphoreType.DMA
    any_space = pl.BlockSpec(memory_space=pl.ANY)
    in_hbm = any_space
    far = n_enc // 2 - (n_enc // 2 + 2) // 3
    scratch = [
        pltpu.SMEM((1, 1, n_enc), jnp.int32),
        vmem((1, features), f32),
        vmem((units, 1, UNIT), f32),
        vmem((n_enc, cap, features), bf16),
        vmem((units, UNIT, columns), bf16),
        vmem((n_enc, cap, columns), bf16),
        vmem((n_enc, cap, columns), bf16),
        vmem((2, far, cap, columns), bf16),
        vmem((units, rows // 8, 8, UNIT), f32),
        vmem((units, rows // 16, 16, UNIT), bf16),
        vmem((rows // 8, 8, LANES), f32),
        vmem((rows // 8, 8, columns), f32),
        vmem((n_enc, cap, columns), bf16),
        vmem((rows // 8, 8, columns), f32),
        vmem((rows // 8, 8, LANES), f32),
        vmem((RING, per_rank, rows, UNIT), bf16),
        vmem((RING, per_rank, rows, UNIT), bf16),
        vmem((RING, per_rank, rows, UNIT), f32),
        vmem((2, per_rank, rows // 2, UNIT), bf16),
        vmem((2, per_rank, rows // 2, UNIT), bf16),
        vmem((2, 2, per_rank, rows // 2, UNIT), bf16),
        vmem((2, 2, per_rank, rows // 2, UNIT), bf16),
        vmem((n_enc, cap, own), bf16),
        vmem((n_llm, n_tp, q_rows, LANES), f32),
        vmem((n_llm, n_tp, q_rows, LANES), f32),
        vmem((q_rows, LANES), f32),
        vmem((q_rows, LANES), f32),
        vmem((n_enc, q_rows, LANES), f32),
        vmem((q_rows, LANES), f32),
        vmem((2, far, cap, columns), bf16),
        *[dma((n_enc,))] * 6,
        *[dma((n_llm, n_tp))] * 2,
        *[dma((n_llm,))] * 2,
        *[dma((2, far))] * 2,
        *[dma((RING,))] * 2,
        *[dma((2,))] * 2,
        *[dma((2, 2))] * 2,
        *[dma((2, far))] * 2,
        dma((9,)),
        pltpu.SemaphoreType.REGULAR,
    ]
    results = (
        jax.ShapeDtypeStruct((1, 1, n_enc, cap, columns), bf16),
        jax.ShapeDtypeStruct((1, 1, n_enc, cap, own), bf16),
        jax.ShapeDtypeStruct((n_llm, q_rows, LANES), f32),
    )
    parts = pl.pallas_call(
        kernel,
        out_shape=results,
        in_specs=[in_hbm] * 6,
        out_specs=[any_space] * 3,
        scratch_shapes=scratch,
        compiler_params=pltpu.CompilerParams(
            collective_id=0, has_side_effects=True, vmem_limit_bytes=48 << 20
        ),
    )(
        *[
            pltpu.with_memory_space_constraint(value, pltpu.HBM)
            for value in (
                counts,
                merger_bias.reshape(1, features),
                norm_gain.reshape(units, 1, UNIT),
                visual,
                kv_weight.reshape(units, UNIT, columns),
                kv_cotangent,
            )
        ]
    )
    key_values, visual_grad, bias_grad = pl.pallas_call(
        write_back,
        out_shape=results,
        in_specs=[any_space] * 3,
        out_specs=[any_space] * 3,
        scratch_shapes=[dma((3,))],
    )(*[pltpu.with_memory_space_constraint(part, pltpu.VMEM) for part in parts])
    return (key_values, visual_grad, bias_grad.reshape(own))


def solution(mesh):
    return jax.shard_map(
        per_device,
        mesh=mesh,
        in_specs=(
            P("enc", "llm", None, None, None),
            P("enc", "llm", None),
            P(),
            P(),
            P(None, "tp"),
            P("enc", "llm", None, None, "tp"),
        ),
        out_specs=(P("enc", "llm", None, None, "tp"), P("enc", "llm", None, None, "tp"), P("tp")),
        check_vma=False,
    )
```
